256 devices in a mesh: dp: 64 (over z, y, core), tensor: 4 (over x).
Axes of the slice: x: 4, y: 4, z: 8, core: 2. Of those that a mesh axis runs over, the one named last changes fastest.
Arguments:
- tokens: bfloat16 [32768, 8192], P('dp', 'tensor'), may hold values from -6 to 6
- token_adapter_index: int32 [32768, 1], P('dp'), may hold values from 0 to 63; in each aligned block of 512 rows (0 to 511, 512 to 1023, ...) at most 16 rows name the same one
- frozen_key_value_weight: bfloat16 [8192, 2048], P('tensor'), may hold values from -0.0625 to 0.0625
- adapter_down_weight: bfloat16 [64, 64, 8192], P('dp', None, 'tensor'), may hold values from -0.0625 to 0.0625
- adapter_up_weight: bfloat16 [64, 64, 2048], P('dp', None, 'tensor'), may hold values from -0.75 to 0.75
Outputs:
- projected: bfloat16 [32768, 2048], P('dp', 'tensor')
The draws below stay inside these ranges and needn't reach their ends.
Inputs may be any that keep to these rules, and one draw needn't show every extreme that they name: `token_adapter_index`: among the tokens of one index of dp, no adapter is named by more than 16 tokens, a bound that some block reaches.
All inputs are finite; a program needn't handle non-finite values.
Results may differ from the reference program's by a relative error of at most 0.0048.
Values may be sent and summed in bfloat16 or wider, within the bound.
No kernel may reach another device: no remote copies, remote signals or barrier semaphores. Data moves between devices by JAX's collectives and lax.ppermute only.
A program may use at most 128 MiB of HBM per device.

```python
import math
import jax
import jax.numpy as jnp
import numpy as np
from jax import lax

MODEL_WIDTH = 8192
KEY_VALUE_WIDTH = 2048
ADAPTER_RANK = 64
TOK_DEV = 512
TOKENS = 32768
ADAPTER_COUNT = 64
CAP = 16
N_DP = 64


def level_of(rng, extent, shards, smallest, top_value):
    def one(position, blocks):
        draws = jax.random.uniform(jax.random.fold_in(jax.random.fold_in(rng, 6), position), (blocks,), jnp.float32, smallest / len(shards), top_value / len(shards))
        return jnp.repeat(jnp.exp(draws), extent[position] // blocks).reshape((-1,) + (1,) * (len(extent) - position - 1))

    level = one(*shards[0])
    for cut in shards[1:]:
        level = level * one(*cut)
    return level


def assign_block(rng, own, number, rows, amount, top, bound, slope):
    order = jax.random.permutation(rng, amount)
    heavy_load, ordinary = portions_of(amount, rows * top, bound, slope, True), portions_of(amount, rows * top, bound, slope, False)
    places = jnp.arange(amount)

    def named(tallies, turn):
        used = int((tallies > 0).sum())
        fixed = max(1, used // 4)
        shifted = fixed + (places - fixed + turn * (used - fixed)) % max(1, amount - fixed)
        return jnp.zeros((amount,), jnp.int32).at[order[jnp.where(places < fixed, places, shifted)]].set(jnp.asarray(tallies, jnp.int32))

    tallies = jnp.where(number % 4 == 0, named(heavy_load, number // 4), named(ordinary, number - number // 4 - 1))
    mixed = jax.random.permutation(jax.random.fold_in(own, 3), amount)
    giver, receiver = mixed[0:amount // 2 * 2:2], mixed[1:amount // 2 * 2:2]
    slack = jnp.minimum(tallies[giver] - 1, bound - tallies[receiver]) // 2
    slack = jnp.where((giver == order[0]) | (receiver == order[0]) | (tallies[receiver] == 0), 0, jnp.maximum(slack, 0))
    shifted = jax.random.randint(jax.random.fold_in(own, 4), (amount // 2,), 0, 1 << 20) % (slack + 1)
    tallies = tallies.at[giver].add(-shifted).at[receiver].add(shifted)
    labels = jnp.searchsorted(jnp.cumsum(tallies), jnp.arange(rows * top), side="right").astype(jnp.int32)
    grid = labels.reshape(top, rows).T
    grid = grid[jax.random.permutation(jax.random.fold_in(own, 1), rows)]
    turn = jax.random.randint(jax.random.fold_in(own, 2), (rows, 1), 0, top)
    return jnp.take_along_axis(grid, (jnp.arange(top)[None, :] + turn) % top, axis=1)


def portions_of(count, total, reach, slope, full):
    weights = [(1 << 20) // math.isqrt(standing ** slope) + 1 for standing in range(1, count + 1)]
    largest = reach if full else min(reach, max(-(-total // count), total * weights[0] // sum(weights)))
    least = 1 if total - largest >= count - 1 else 0
    holding, surplus = [largest] + [least] * (count - 1), total - largest - least * (count - 1)
    while surplus > 0:
        movable = [i for i in range(1, count) if holding[i] < largest] or [i for i in range(1, count) if holding[i] < reach]
        mass, remaining = sum([weights[i] for i in movable]), surplus
        for i in movable:
            addition = min(reach - holding[i], max(1, remaining * weights[i] // mass), surplus)
            holding[i] = holding[i] + addition
            surplus = surplus - addition
    return np.array(holding)


def scatter_about(key, dims, spread, most, split=(), kind=jnp.bfloat16):
    gain = level_of(key, dims, split, -0.22, 0.18) if split else 1.0
    entries = jax.random.normal(key, dims, jnp.float32) * spread * gain
    return jnp.minimum(jnp.maximum(entries, -most), most).astype(kind)


def setup_inputs(seed: int = 0) -> dict:
    key_of = jax.random.split(jax.random.key(seed), 6)
    tokens = scatter_about(key_of[0], (TOKENS, MODEL_WIDTH), 1.0, 6.0, ((0, 64), (1, 4)))
    token_adapter_index_keys = jax.random.split(jax.random.fold_in(key_of[1], 1), TOKENS // TOK_DEV)
    token_adapter_index_turns = jax.random.permutation(jax.random.fold_in(key_of[1], 3), TOKENS // TOK_DEV)
    token_adapter_index = jax.vmap(lambda own, number: assign_block(jax.random.fold_in(key_of[1], 2), own, number, TOK_DEV, ADAPTER_COUNT, 1, CAP, 1))(token_adapter_index_keys, token_adapter_index_turns).reshape((TOKENS, 1))
    frozen_key_value_weight = scatter_about(key_of[2], (MODEL_WIDTH, KEY_VALUE_WIDTH), MODEL_WIDTH ** -0.5, 0.0625, ((0, 4),))
    adapter_down_weight = scatter_about(key_of[3], (ADAPTER_COUNT, ADAPTER_RANK, MODEL_WIDTH), MODEL_WIDTH ** -0.5, 0.0625, ((0, 64), (2, 4)))
    adapter_up_weight = scatter_about(key_of[4], (ADAPTER_COUNT, ADAPTER_RANK, KEY_VALUE_WIDTH), ADAPTER_RANK ** -0.5, 0.75, ((0, 64), (2, 4)))
    return dict(tokens=tokens, token_adapter_index=token_adapter_index, frozen_key_value_weight=frozen_key_value_weight, adapter_down_weight=adapter_down_weight, adapter_up_weight=adapter_up_weight)


def reference(tokens, token_adapter_index, frozen_key_value_weight, adapter_down_weight, adapter_up_weight):
    adapter_of = token_adapter_index[:, 0]
    base_out = jnp.dot(tokens, frozen_key_value_weight, preferred_element_type=jnp.float32)
    permuted = jnp.argsort(adapter_of, stable=True).astype(jnp.int32)
    inverse = jnp.argsort(permuted, stable=True).astype(jnp.int32)
    matches = adapter_of[None, :] == jnp.arange(ADAPTER_COUNT, dtype=jnp.int32)[:, None]
    counts = jnp.sum(matches.astype(jnp.int32), axis=1).astype(jnp.int32)
    starts = (jnp.cumsum(counts) - counts).astype(jnp.int32)
    window = N_DP * CAP
    sorted_rows = jnp.concatenate([tokens[permuted], jnp.zeros((window, MODEL_WIDTH), tokens.dtype)], axis=0)

    def visit_adapter(sorted_delta, adapter_number):
        first_row = starts[adapter_number]
        token_block_rows = lax.dynamic_slice_in_dim(sorted_rows, first_row, window, 0)
        reduced_activations = jnp.dot(token_block_rows, adapter_down_weight[adapter_number].T, preferred_element_type=jnp.float32).astype(jnp.bfloat16)
        adapter_delta = jnp.dot(reduced_activations, adapter_up_weight[adapter_number], preferred_element_type=jnp.float32).astype(jnp.bfloat16)
        active_token_rows = (jnp.arange(window, dtype=jnp.int32) < counts[adapter_number])[:, None]
        prior_output = lax.dynamic_slice_in_dim(sorted_delta, first_row, window, 0)
        refreshed_output = jnp.where(active_token_rows, adapter_delta, prior_output)
        return lax.dynamic_update_slice_in_dim(sorted_delta, refreshed_output, first_row, 0), None

    initial = jnp.zeros((TOKENS + window, KEY_VALUE_WIDTH), jnp.bfloat16)
    sorted_delta, unused = lax.scan(visit_adapter, initial, jnp.arange(ADAPTER_COUNT, dtype=jnp.int32))
    token_delta = sorted_delta[inverse]
    return (base_out + token_delta.astype(jnp.float32)).astype(jnp.bfloat16)
```

```python
import functools

import jax
import jax.numpy as jnp
from jax import lax
from jax.experimental import pallas as pl
from jax.experimental.pallas import tpu as pltpu
from jax.sharding import Mesh, PartitionSpec as P

F32 = jnp.float32
BF16 = jnp.bfloat16
NZ, NY, NC, NX = 8, 4, 2, 4
GROUP = ("y", "core")
VMEM_LIMIT = 48 * 1024 * 1024
RELATIVE_Z = (0, -1, 1, -2, 2, -3, 3, -4)


def ring(size, step):
    return [(place, (place + step) % size) for place in range(size)]


def estimate(flops, moved):
    return pl.CostEstimate(flops=flops, bytes_accessed=moved, transcendentals=0)


def base_kernel(which, tokens, weight, out, total):
    step = pl.program_id(1)

    @pl.when(step == 0)
    def _():
        total[...] = jnp.zeros_like(total)

    total[...] += jnp.dot(tokens[...], weight[...], preferred_element_type=F32)

    @pl.when(step == pl.num_programs(1) - 1)
    def _():
        out[0] = total[...].astype(out.dtype)


def base_chunks(tokens, weight, which, dtype, depth=512):
    count, inner = tokens.shape
    width = weight.shape[1] // NX
    chunks = which.shape[0]
    return pl.pallas_call(
        base_kernel,
        out_shape=jax.ShapeDtypeStruct((chunks, count, width), dtype),
        grid_spec=pltpu.PrefetchScalarGridSpec(
            num_scalar_prefetch=1,
            grid=(chunks, inner // depth),
            in_specs=[
                pl.BlockSpec((count, depth), lambda j, k, w: (0, k)),
                pl.BlockSpec((depth, width), lambda j, k, w: (k, w[j])),
            ],
            out_specs=pl.BlockSpec((1, count, width), lambda j, k, w: (j, 0, 0)),
            scratch_shapes=[pltpu.VMEM((count, width), F32)],
        ),
        compiler_params=pltpu.CompilerParams(vmem_limit_bytes=VMEM_LIMIT),
        cost_estimate=estimate(2 * chunks * count * inner * width, 4 * chunks * inner * width),
        name="base",
    )(which, tokens, weight)


def down_kernel(chunks, first, last, starts, tokens, owner, *refs):
    panels, refs = refs[:chunks], refs[chunks:]
    if first:
        (out,) = refs
    else:
        before, out = refs
    value = tokens[0]
    named = owner[0]
    lane = lax.broadcasted_iota(jnp.int32, (1, 128), 1) // 64
    total = jnp.zeros((value.shape[0], 128), F32)
    if not first:
        total = before[0].astype(F32)
    for i in range(chunks):
        panel = panels[i][...].reshape(8 * 64, value.shape[1])
        product = lax.dot_general(
            value, panel, (((1,), (1,)), ((), ())), preferred_element_type=F32
        )
        for k in range(4):
            here = named == starts[i] + 2 * k + lane
            total = total + jnp.where(here, product[:, 128 * k : 128 * k + 128], 0.0)
    if last:
        total = total + pltpu.roll(total, 64, 1)
        half = total.shape[0] // 2
        total = jnp.where(lane == 0, total[:half], total[half:])
    out[0] = total.astype(out.dtype)


def down_step(starts, tokens, owner, panels, before, last):
    sources, count, width = tokens.shape
    chunks, first = len(panels), before is None
    rows = count // 2 if last else count
    state = [] if first else [before]
    return pl.pallas_call(
        functools.partial(down_kernel, chunks, first, last),
        out_shape=jax.ShapeDtypeStruct((sources, rows, 128), BF16),
        grid_spec=pltpu.PrefetchScalarGridSpec(
            num_scalar_prefetch=1,
            grid=(sources,),
            in_specs=[
                pl.BlockSpec((1, count, width), lambda s, w: (s, 0, 0)),
                pl.BlockSpec((1, count, 1), lambda s, w: (s, 0, 0)),
            ]
            + [pl.BlockSpec((8, 64, width), lambda s, w: (0, 0, 0))] * chunks
            + [pl.BlockSpec((1, count, 128), lambda s, w: (s, 0, 0))] * len(state),
            out_specs=pl.BlockSpec((1, rows, 128), lambda s, w: (s, 0, 0)),
        ),
        compiler_params=pltpu.CompilerParams(vmem_limit_bytes=VMEM_LIMIT),
        cost_estimate=estimate(
            2 * sources * count * width * 512 * chunks, 2 * sources * count * (width + 128)
        ),
        name="down",
    )(starts, tokens, owner, *panels, *state)


def up_kernel(numbers, owner, low, *refs):
    panels, (keep, fore_a, back_a, fore_b, back_b, out) = refs[: NY * NC], refs[NY * NC :]
    total = low[0].astype(F32)
    for i in range(1, NX):
        total = total + low[i].astype(F32)
    total = total.astype(BF16).astype(F32)
    lane = lax.broadcasted_iota(jnp.int32, (1, 128), 1)
    turned = pltpu.roll(total, 64, 1)
    both = jnp.concatenate(
        [jnp.where(lane < 64, total, turned), jnp.where(lane < 64, turned, total)], axis=0
    )
    named = owner[...]
    delta = jnp.zeros(out.shape, F32)
    for k in range(NY * NC):
        parts = []
        for m in range(NZ // 2):
            number = jnp.where(
                lane < 64, numbers[NZ * k + 2 * m], numbers[NZ * k + 2 * m + 1]
            )
            parts.append(jnp.where(named == number, both, 0.0).astype(BF16))
        left = jnp.concatenate(parts, axis=1)
        delta = delta + jnp.dot(left, panels[k][...], preferred_element_type=F32)
    delta = delta.astype(BF16).astype(F32)
    half = out.shape[0] // 2
    top = keep[:half] + fore_b[...].astype(F32) + back_a[...].astype(F32)
    bottom = keep[half:] + fore_a[...].astype(F32) + back_b[...].astype(F32)
    out[:half] = (top + delta[:half]).astype(out.dtype)
    out[half:] = (bottom + delta[half:]).astype(out.dtype)


def up_step(numbers, owner, low, panels, base):
    count = owner.shape[0]
    width = panels[0].shape[1]
    spec = pl.BlockSpec(memory_space=pltpu.VMEM)
    return pl.pallas_call(
        up_kernel,
        out_shape=jax.ShapeDtypeStruct((count, width), BF16),
        in_specs=[pl.BlockSpec(memory_space=pltpu.SMEM)] + [spec] * (2 + len(panels) + len(base)),
        out_specs=spec,
        compiler_params=pltpu.CompilerParams(vmem_limit_bytes=VMEM_LIMIT),
        cost_estimate=estimate(2 * count * width * 4096, 2 * width * 4096),
        name="up",
    )(numbers, owner, low, *panels, *base)


def z_ring(chunk):
    fore = back = chunk
    found = [chunk]
    for step in range(1, 5):
        fore = lax.ppermute(fore, "z", ring(NZ, 1))
        found.append(fore)
        if step < 4:
            back = lax.ppermute(back, "z", ring(NZ, -1))
            found.append(back)
    return found


def on_device(tokens, owner, weight, down, up):
    z, y, core, x = (lax.axis_index(name) for name in ("z", "y", "core", "x"))
    count, inner = tokens.shape
    size = NY * NC
    width = inner // size
    rank = down.shape[1]

    marks = jnp.zeros((16 * width,), BF16).at[:count].set(owner[:, 0].astype(BF16))
    marks = jnp.broadcast_to(marks.reshape(1, 16, width), (size, 16, width))
    spread = jnp.concatenate([down[0].reshape(rank, size, width).transpose(1, 0, 2), marks], axis=1)
    spread = lax.all_to_all(spread, GROUP, 0, 0, tiled=True)
    owners = spread[:, rank:].reshape(size, 16 * width)[:, :count, None].astype(jnp.int32)
    mine = spread[:, :rank]

    shared = tokens.reshape(count, size, width).transpose(1, 0, 2)
    shared = lax.all_to_all(shared, GROUP, 0, 0, tiled=True)

    two = base_chunks(tokens, weight, ((x + 2) % NX)[None], BF16)[0]
    rest = base_chunks(tokens, weight, jnp.stack([(x + 1) % NX, (x + 3) % NX, x]), F32)
    half = count // 2
    fore = lax.ppermute(two[:half], "x", ring(NX, 1))
    back = lax.ppermute(two[half:], "x", ring(NX, -1))
    fore_a = lax.ppermute(rest[0, half:].astype(BF16), "x", ring(NX, 1))
    back_a = lax.ppermute(rest[1, :half].astype(BF16), "x", ring(NX, -1))
    fore_b = lax.ppermute((rest[0, :half] + fore.astype(F32)).astype(BF16), "x", ring(NX, 1))
    back_b = lax.ppermute((rest[1, half:] + back.astype(F32)).astype(BF16), "x", ring(NX, -1))

    column = jnp.concatenate(z_ring(up[0]), axis=0)
    columns = [column] + [lax.ppermute(column, "y", ring(NY, -step)) for step in (1, 2, 3)]
    columns += [lax.ppermute(value, "core", ring(NC, 1)) for value in columns]
    numbers = jnp.stack(
        [
            ((z + dz) % NZ) * size + ((y + dy) % NY) * NC + (core + dc) % NC
            for dc in range(NC)
            for dy in range(NY)
            for dz in RELATIVE_Z
        ]
    )

    panels = z_ring(mine)
    starts = [((z + dz) % NZ) * size for dz in RELATIVE_Z]
    state = None
    for low, high in ((0, 1), (1, 3), (3, 5), (5, 7), (7, 8)):
        state = down_step(
            jnp.stack(starts[low:high]), shared, owners, panels[low:high], state, high == NZ
        )
    state = lax.all_to_all(state, GROUP, 0, 0, tiled=True)
    part = jnp.sum(state.astype(F32), axis=0).astype(BF16)
    parts = [part] + [lax.ppermute(part, "x", ring(NX, step)) for step in (1, 2, 3)]
    return up_step(
        numbers, owner, jnp.stack(parts), columns, (rest[2], fore_a, back_a, fore_b, back_b)
    )


def solution(mesh):
    fine = Mesh(mesh.devices.reshape(NZ, NY, NC, NX), ("z", "y", "core", "x"))
    dp = ("z", "y", "core")
    placed = (P(dp, "x"), P(dp, None), P("x", None), P(dp, None, "x"), P(dp, None, "x"))
    return jax.shard_map(
        on_device, mesh=fine, in_specs=placed, out_specs=P(dp, "x"), check_vma=False
    )
```

```python
import jax
import jax.numpy as jnp
from jax import lax
from jax.experimental import pallas as pl
from jax.experimental.pallas import tpu as pltpu
from jax.sharding import Mesh, PartitionSpec as P

F32 = jnp.float32
BF16 = jnp.bfloat16
NZ, NY, NC, NX = 8, 4, 2, 4
COLUMNS = NY * NC
CAP = 16
GROUP = ("y", "core")
VMEM_LIMIT = 48 * 1024 * 1024
RELATIVE_Z = (0, -1, 1, -2, 2, -3, 3, -4)


def ring(size, step):
    return [(place, (place + step) % size) for place in range(size)]


def call(kernel, name, out, grid, ins, outs, flops, moved, prefetch=0, scratch=()):
    return pl.pallas_call(
        kernel,
        out_shape=out,
        grid_spec=pltpu.PrefetchScalarGridSpec(
            num_scalar_prefetch=prefetch,
            grid=grid,
            in_specs=ins,
            out_specs=outs,
            scratch_shapes=scratch,
        ),
        compiler_params=pltpu.CompilerParams(vmem_limit_bytes=VMEM_LIMIT),
        cost_estimate=pl.CostEstimate(flops=flops, bytes_accessed=moved, transcendentals=0),
        name=name,
    )


def base_kernel(which, tokens, weight, out):
    out[0] = jnp.dot(tokens[...], weight[...], preferred_element_type=F32).astype(out.dtype)


def base_chunks(tokens, weight, which, dtype, tile=256):
    count, inner = tokens.shape
    width = weight.shape[1] // NX
    chunks = which.shape[0]
    tiles = width // tile
    return call(
        base_kernel,
        "base",
        jax.ShapeDtypeStruct((chunks, count, width), dtype),
        (chunks, tiles),
        [
            pl.BlockSpec((count, inner), lambda j, n, w: (0, 0)),
            pl.BlockSpec((inner, tile), lambda j, n, w: (0, w[j] * tiles + n)),
        ],
        pl.BlockSpec((1, count, tile), lambda j, n, w: (j, 0, n)),
        2 * chunks * count * inner * width,
        2 * (count + chunks * width) * inner,
        prefetch=1,
    )(which, tokens, weight)


def dispatch_kernel(named, owner, tokens, out, place):
    count = tokens.shape[0]

    @pl.when(pl.program_id(0) == 0)
    def _():
        mine = owner[...]
        above = lax.broadcasted_iota(jnp.int32, (count, count), 0)
        below = lax.broadcasted_iota(jnp.int32, (count, count), 1)
        earlier = (named[...] == mine) & (above < below)
        position = jnp.sum(earlier.astype(jnp.int32), axis=0, keepdims=True)
        place[...] = (mine % COLUMNS) * (NZ * CAP) + (mine // COLUMNS) * CAP + position

    rows = out.shape[1]
    slot = lax.broadcasted_iota(jnp.int32, (rows, count), 0) + pl.program_id(0) * rows
    chosen = (slot == place[...]).astype(BF16)
    out[0] = jnp.dot(chosen, tokens[...], preferred_element_type=F32).astype(BF16)


def dispatch(tokens, owner):
    count, inner = tokens.shape
    rows = NZ * CAP
    return call(
        dispatch_kernel,
        "dispatch",
        jax.ShapeDtypeStruct((COLUMNS, rows, inner), BF16),
        (COLUMNS,),
        [
            pl.BlockSpec((count, 1), lambda d: (0, 0)),
            pl.BlockSpec((1, count), lambda d: (0, 0)),
            pl.BlockSpec((count, inner), lambda d: (0, 0)),
        ],
        pl.BlockSpec((1, rows, inner), lambda d: (d, 0, 0)),
        2 * COLUMNS * rows * count * inner,
        2 * (count + COLUMNS * rows) * inner,
        scratch=[pltpu.VMEM((1, count), jnp.int32)],
    )(owner, owner.reshape(1, count), tokens)


def down_kernel(order, rows, *refs):
    panels, out = refs[:NZ], refs[NZ]
    inner = rows.shape[2]
    value = rows[...].reshape(COLUMNS * CAP, inner)
    for i in range(NZ):

        @pl.when(pl.program_id(0) == i)
        def _():
            product = lax.dot_general(
                value,
                panels[i][:, :inner],
                (((1,), (1,)), ((), ())),
                preferred_element_type=F32,
            )
            half = product.shape[0] // 2
            out[0] = jnp.concatenate([product[:half], product[half:]], axis=1).astype(BF16)


def down_step(order, rows, panels):
    inner = rows.shape[2]
    rank, wide = panels[0].shape
    lines = COLUMNS * CAP // 2
    return call(
        down_kernel,
        "down",
        jax.ShapeDtypeStruct((NZ, lines, 2 * rank), BF16),
        (NZ,),
        [pl.BlockSpec((COLUMNS, CAP, inner), lambda i, o: (0, o[i], 0))]
        + [pl.BlockSpec((rank, wide), lambda i, o: (0, 0))] * NZ,
        pl.BlockSpec((1, lines, 2 * rank), lambda i, o: (i, 0, 0)),
        4 * NZ * lines * inner * rank,
        2 * NZ * (2 * lines + rank) * inner,
        prefetch=1,
    )(order, rows, *panels)


def up_kernel(order, *refs):
    parts, panels, out = refs[:NX], refs[NX : NX + NZ], refs[NX + NZ]
    total = parts[0][0].astype(F32)
    for part in parts[1:]:
        total = total + part[0].astype(F32)
    rank = total.shape[1] // 2
    low = jnp.concatenate([total[:, :rank], total[:, rank:]], axis=0).astype(BF16)
    for i in range(NZ):

        @pl.when(pl.program_id(0) == i)
        def _():
            width = out.shape[2]
            panel = panels[i][:, panels[i].shape[1] - width :]
            delta = jnp.dot(low, panel, preferred_element_type=F32)
            out[...] = delta.astype(BF16).reshape(out.shape)


def up_step(order, parts, panels, width):
    rank, wide = panels[0].shape
    lines = COLUMNS * CAP // 2
    return call(
        up_kernel,
        "up",
        jax.ShapeDtypeStruct((COLUMNS, NZ * CAP, width), BF16),
        (NZ,),
        [pl.BlockSpec((1, lines, 2 * rank), lambda i, o: (i, 0, 0))] * NX
        + [pl.BlockSpec((rank, wide), lambda i, o: (0, 0))] * NZ,
        pl.BlockSpec((COLUMNS, CAP, width), lambda i, o: (0, o[i], 0)),
        4 * NZ * lines * rank * width,
        2 * NZ * (2 * lines + rank) * width,
        prefetch=1,
    )(order, *parts, *panels)


def final_kernel(place, delta, keep, fore_a, back_a, fore_b, back_b, out):
    count = out.shape[0]
    slots = delta.shape[0]
    chosen = (lax.broadcasted_iota(jnp.int32, (count, slots), 1) == place[...]).astype(BF16)
    mine = jnp.dot(chosen, delta[...], preferred_element_type=F32)
    half = count // 2
    top = keep[:half] + fore_b[...].astype(F32) + back_a[...].astype(F32)
    bottom = keep[half:] + fore_a[...].astype(F32) + back_b[...].astype(F32)
    out[:half] = (top + mine[:half]).astype(out.dtype)
    out[half:] = (bottom + mine[half:]).astype(out.dtype)


def final_step(place, delta, base):
    count = place.shape[0]
    slots, width = delta.shape
    tile = 256
    half = pl.BlockSpec((count // 2, tile), lambda n: (0, n))
    return call(
        final_kernel,
        "final",
        jax.ShapeDtypeStruct((count, width), BF16),
        (width // tile,),
        [
            pl.BlockSpec((count, 1), lambda n: (0, 0)),
            pl.BlockSpec((slots, tile), lambda n: (0, n)),
            pl.BlockSpec((count, tile), lambda n: (0, n)),
            half,
            half,
            half,
            half,
        ],
        pl.BlockSpec((count, tile), lambda n: (0, n)),
        2 * count * slots * width,
        2 * (slots + 4 * count) * width,
    )(place, delta, *base)


def z_ring(chunk):
    fore = back = chunk
    found = [chunk]
    for step in range(1, 5):
        fore = lax.ppermute(fore, "z", ring(NZ, 1))
        found.append(fore)
        if step < 4:
            back = lax.ppermute(back, "z", ring(NZ, -1))
            found.append(back)
    return found


def on_device(tokens, owner, weight, down, up):
    z, x = lax.axis_index("z"), lax.axis_index("x")
    count = tokens.shape[0]
    half = count // 2

    rows = lax.all_to_all(dispatch(tokens, owner), GROUP, 0, 0, tiled=True)
    panels = z_ring(jnp.concatenate([down[0], up[0]], axis=1))
    order = jnp.stack([(z + dz) % NZ for dz in RELATIVE_Z])

    two = base_chunks(tokens, weight, ((x + 2) % NX)[None], BF16)[0]
    rest = base_chunks(tokens, weight, jnp.stack([(x + 1) % NX, (x + 3) % NX, x]), F32)
    fore = lax.ppermute(two[:half], "x", ring(NX, 1))
    back = lax.ppermute(two[half:], "x", ring(NX, -1))
    fore_a = lax.ppermute(rest[0, half:].astype(BF16), "x", ring(NX, 1))
    back_a = lax.ppermute(rest[1, :half].astype(BF16), "x", ring(NX, -1))
    fore_b = lax.ppermute((rest[0, :half] + fore.astype(F32)).astype(BF16), "x", ring(NX, 1))
    back_b = lax.ppermute((rest[1, half:] + back.astype(F32)).astype(BF16), "x", ring(NX, -1))

    named = owner[:, 0]
    turn = jnp.arange(count, dtype=jnp.int32)
    earlier = (named[None, :] == named[:, None]) & (turn[None, :] < turn[:, None])
    position = jnp.sum(earlier.astype(jnp.int32), axis=1)
    place = (named % COLUMNS) * (NZ * CAP) + (named // COLUMNS) * CAP + position

    part = down_step(order, rows, panels)
    parts = [part] + [lax.ppermute(part, "x", ring(NX, step)) for step in (1, 2, 3)]
    delta = up_step(order, parts, panels, up.shape[2])
    delta = lax.all_to_all(delta, GROUP, 0, 0, tiled=True)
    return final_step(
        place[:, None],
        delta.reshape(COLUMNS * NZ * CAP, up.shape[2]),
        (rest[2], fore_a, back_a, fore_b, back_b),
    )


def solution(mesh):
    fine = Mesh(mesh.devices.reshape(NZ, NY, NC, NX), ("z", "y", "core", "x"))
    dp = ("z", "y", "core")
    placed = (P(dp, "x"), P(dp, None), P("x", None), P(dp, None, "x"), P(dp, None, "x"))
    return jax.shard_map(
        on_device, mesh=fine, in_specs=placed, out_specs=P(dp, "x"), check_vma=False
    )
```

```python
import jax
import jax.numpy as jnp
from jax import lax
from jax.experimental import pallas as pl
from jax.experimental.pallas import tpu as pltpu
from jax.sharding import Mesh, PartitionSpec as P

F32 = jnp.float32
BF16 = jnp.bfloat16
NZ, NY, NC, NX = 8, 4, 2, 4
COLUMNS = NY * NC
CAP = 16
GROUP = ("y", "core")
WHOLE, PART = 60, 16
ROUTES = ((2, 0), (2, 1), (1, 0), (3, 0), (1, 1), (3, 1), (0, 1))
RELATIVE_Z = (0, -1, 1, -2, 2, -3, 3, -4)


def ring(size, step):
    return [(place, (place + step) % size) for place in range(size)]


def call(kernel, name, out, grid, ins, outs, flops, moved, limit, prefetch=0, scratch=()):
    return pl.pallas_call(
        kernel,
        out_shape=out,
        grid_spec=pltpu.PrefetchScalarGridSpec(
            num_scalar_prefetch=prefetch,
            grid=grid,
            in_specs=ins,
            out_specs=outs,
            scratch_shapes=scratch,
        ),
        compiler_params=pltpu.CompilerParams(vmem_limit_bytes=limit * 1024 * 1024),
        cost_estimate=pl.CostEstimate(flops=flops, bytes_accessed=moved, transcendentals=0),
        name=name,
    )


def base_kernel(which, tokens, weight, *outs):
    product = jnp.dot(tokens[...], weight[...], preferred_element_type=F32)
    half = product.shape[0] // 2
    for j in range(2):

        @pl.when(pl.program_id(0) == j)
        def _():
            top, bottom = outs[2 * j : 2 * j + 2]
            top[...] = product[:half].astype(top.dtype)
            bottom[...] = product[half:].astype(bottom.dtype)


def base_pair(tokens, weight, which, types, tile=256):
    count, inner = tokens.shape
    width = weight.shape[1] // NX
    tiles = width // tile
    first = pl.BlockSpec((count // 2, tile), lambda j, n, w: (0, n + j * (tiles - 1 - n)))
    second = pl.BlockSpec((count // 2, tile), lambda j, n, w: (0, n * j))
    return call(
        base_kernel,
        "base",
        [jax.ShapeDtypeStruct((count // 2, width), kind) for kind in types],
        (2, tiles),
        [
            pl.BlockSpec((count, inner), lambda j, n, w: (0, 0)),
            pl.BlockSpec((inner, tile), lambda j, n, w: (0, w[j] * tiles + n)),
        ],
        [first, first, second, second],
        4 * count * inner * width,
        2 * (count + 2 * width) * inner,
        WHOLE,
        prefetch=1,
    )(jnp.stack(which), tokens, weight)


def dispatch_kernel(owner, tokens, out, chosen, held, made, taken, given):
    count = held.shape[0]
    slots = chosen.shape[0]
    fetch = pltpu.make_async_copy(tokens, held, taken)
    fetch.start()
    mine = owner[...]
    adapter = lax.broadcasted_iota(jnp.int32, (NZ * COLUMNS, count), 0)
    member = (adapter == mine).astype(F32)
    above = lax.broadcasted_iota(jnp.int32, (count, count), 0)
    below = lax.broadcasted_iota(jnp.int32, (count, count), 1)
    before = (above < below).astype(F32).astype(BF16)
    earlier = jnp.dot(member.astype(BF16), before, preferred_element_type=F32)
    position = jnp.sum(earlier * member, axis=0, keepdims=True).astype(jnp.int32)
    place = (mine % COLUMNS) * (NZ * CAP) + (mine // COLUMNS) * CAP + position
    slot = lax.broadcasted_iota(jnp.int32, (slots, count), 0)
    chosen[...] = (slot == place).astype(F32).astype(BF16)
    fetch.wait()
    copies = []
    rows = slots // 4
    for part in range(4):
        block = made.at[pl.ds(2 * part, 2)]
        product = jnp.dot(
            chosen[part * rows : (part + 1) * rows], held[...], preferred_element_type=F32
        )
        block[...] = product.astype(BF16).reshape(block.shape)
        copy = pltpu.make_async_copy(block, out.at[pl.ds(2 * part, 2)], given.at[part])
        copy.start()
        copies.append(copy)
    for copy in copies:
        copy.wait()


def dispatch(tokens, owner):
    count, inner = tokens.shape
    rows = NZ * CAP
    whole = pl.BlockSpec(memory_space=pl.ANY)
    return call(
        dispatch_kernel,
        "dispatch",
        jax.ShapeDtypeStruct((COLUMNS, rows, inner), BF16),
        (1,),
        [pl.BlockSpec((1, count), lambda n: (0, 0)), whole],
        whole,
        2 * COLUMNS * rows * count * inner,
        2 * (count + COLUMNS * rows) * inner,
        WHOLE,
        scratch=[
            pltpu.VMEM((COLUMNS * rows, count), BF16),
            pltpu.VMEM((count, inner), BF16),
            pltpu.VMEM((COLUMNS, rows, inner), BF16),
            pltpu.SemaphoreType.DMA,
            pltpu.SemaphoreType.DMA((4,)),
        ],
    )(owner.reshape(1, count), tokens)


def down_kernel(order, rows, *refs):
    panels, (out, held, kept, first, second) = refs[:NZ], refs[NZ:]
    inner = rows.shape[2]
    copies = []
    for i in range(NZ):
        start = pl.multiple_of(order[i] * CAP, CAP)
        pair = (
            pltpu.make_async_copy(rows.at[:, pl.ds(start, CAP), :], held.at[i], first.at[i]),
            pltpu.make_async_copy(panels[i].at[:, pl.ds(0, inner)], kept.at[i], second.at[i]),
        )
        for copy in pair:
            copy.start()
        copies.append(pair)
    many, rank = 4, kept.shape[1]
    lines = COLUMNS * CAP
    for start in range(0, NZ, many):
        for pair in copies[start : start + many]:
            for copy in pair:
                copy.wait()
        product = lax.dot_general(
            held[start : start + many].reshape(many * lines, inner),
            kept[start : start + many].reshape(many * rank, inner),
            (((1,), (1,)), ((), ())),
            preferred_element_type=F32,
        )
        for i in range(many):
            block = product[i * lines : (i + 1) * lines, i * rank : (i + 1) * rank]
            half = lines // 2
            out[start + i] = jnp.concatenate([block[:half], block[half:]], axis=1).astype(BF16)


def down_step(order, rows, panels):
    inner = rows.shape[2]
    rank = panels[0].shape[0]
    lines = COLUMNS * CAP // 2
    whole = pl.BlockSpec(memory_space=pl.ANY)
    return call(
        down_kernel,
        "down",
        jax.ShapeDtypeStruct((NZ, lines, 2 * rank), BF16),
        (1,),
        [whole] * (1 + NZ),
        pl.BlockSpec((NZ, lines, 2 * rank), lambda i, o: (0, 0, 0)),
        4 * NZ * lines * inner * rank,
        2 * NZ * (2 * lines + rank) * inner,
        WHOLE,
        prefetch=1,
        scratch=[
            pltpu.VMEM((NZ, COLUMNS, CAP, inner), BF16),
            pltpu.VMEM((NZ, rank, inner), BF16),
            pltpu.SemaphoreType.DMA((NZ,)),
            pltpu.SemaphoreType.DMA((NZ,)),
        ],
    )(order, rows, *panels)


def up_kernel(order, homes, *refs):
    parts, panels, outs, low = refs[:NX], refs[NX : NX + NZ], refs[NX + NZ : -1], refs[-1]
    for i in range(NZ):
        total = parts[0][i].astype(F32)
        for part in parts[1:]:
            total = total + part[i].astype(F32)
        rank = total.shape[1] // 2
        low[...] = jnp.concatenate([total[:, :rank], total[:, rank:]], axis=0)
        picked = [
            low[pl.ds(pl.multiple_of(homes[r] * CAP, CAP), CAP), :] for r in range(COLUMNS)
        ]
        delta = jnp.dot(
            jnp.concatenate(picked, axis=0).astype(BF16),
            panels[i][...],
            preferred_element_type=F32,
        ).astype(BF16)
        start = pl.multiple_of(order[i] * CAP, CAP)
        for r in range(COLUMNS):
            outs[r][pl.ds(start, CAP), :] = delta[r * CAP : (r + 1) * CAP]


def up_step(order, homes, parts, panels, width):
    rank, wide = panels[0].shape
    lines = COLUMNS * CAP // 2
    last = wide // width - 1
    return call(
        up_kernel,
        "up",
        [jax.ShapeDtypeStruct((NZ * CAP, width), BF16)] * COLUMNS,
        (1,),
        [pl.BlockSpec((NZ, lines, 2 * rank), lambda i, o, h: (0, 0, 0))] * NX
        + [pl.BlockSpec((rank, width), lambda i, o, h: (0, last))] * NZ,
        [pl.BlockSpec((NZ * CAP, width), lambda i, o, h: (0, 0))] * COLUMNS,
        4 * NZ * lines * rank * width,
        2 * NZ * (2 * lines + rank) * width,
        WHOLE,
        prefetch=2,
        scratch=[pltpu.VMEM((2 * lines, rank), F32)],
    )(order, homes, *parts, *panels)


def final_kernel(handlers, place, base, *refs):
    pieces, (out, held, kept, arrived) = refs[:COLUMNS], refs[COLUMNS:]
    rows = pieces[0].shape[0]
    copies = [pltpu.make_async_copy(base, kept, arrived.at[COLUMNS])]
    for r in range(COLUMNS):
        start = pl.multiple_of(handlers[r] * rows, rows)
        copies.append(
            pltpu.make_async_copy(pieces[r], held.at[pl.ds(start, rows)], arrived.at[r])
        )
    for copy in copies:
        copy.start()
    count = out.shape[0]
    slots = held.shape[0]
    slot = lax.broadcasted_iota(jnp.int32, (count, slots), 1)
    chosen = (slot == place[...]).astype(F32).astype(BF16)
    for copy in copies:
        copy.wait()
    mine = jnp.dot(chosen, held[...], preferred_element_type=F32)
    out[...] = (kept[...] + mine).astype(out.dtype)


def final_step(handlers, place, pieces, base):
    count = place.shape[0]
    rows, width = pieces[0].shape
    slots = COLUMNS * rows
    whole = pl.BlockSpec(memory_space=pl.ANY)
    return call(
        final_kernel,
        "final",
        jax.ShapeDtypeStruct((count, width), BF16),
        (1,),
        [pl.BlockSpec((count, 1), lambda n, h: (0, 0)), whole] + [whole] * COLUMNS,
        pl.BlockSpec((count, width), lambda n, h: (0, 0)),
        2 * count * slots * width,
        2 * (slots + 4 * count) * width,
        PART,
        prefetch=1,
        scratch=[
            pltpu.VMEM((slots, width), BF16),
            pltpu.VMEM((count, width), F32),
            pltpu.SemaphoreType.DMA((COLUMNS + 1,)),
        ],
    )(handlers, place, base, *pieces)


def group_shift(dy, dc):
    return [
        (y * NC + core, (y + dy) % NY * NC + (core + dc) % NC)
        for y in range(NY)
        for core in range(NC)
    ]


def z_ring(chunk):
    fore = back = chunk
    found = [chunk]
    for step in range(1, 5):
        fore = lax.ppermute(fore, "z", ring(NZ, 1))
        found.append(fore)
        if step < 4:
            back = lax.ppermute(back, "z", ring(NZ, -1))
            found.append(back)
    return found


def on_device(tokens, owner, weight, down, up):
    z, x = lax.axis_index("z"), lax.axis_index("x")
    count = tokens.shape[0]

    rows = lax.all_to_all(dispatch(tokens, owner), GROUP, 0, 0, tiled=True)
    panels = z_ring(jnp.concatenate([down[0], up[0]], axis=1))
    order = jnp.stack([(z + dz) % NZ for dz in RELATIVE_Z])

    fore, back, ahead, sent = base_pair(
        tokens, weight, [(x + 2) % NX, (x + 1) % NX], (BF16, BF16, F32, BF16)
    )
    tokens, fore = lax.optimization_barrier((tokens, fore))
    given, behind, top, bottom = base_pair(
        tokens, weight, [(x + 3) % NX, x], (BF16, F32, F32, F32)
    )
    fore = lax.ppermute(fore, "x", ring(NX, 1))
    back = lax.ppermute(back, "x", ring(NX, -1))
    fore_a = lax.ppermute(sent, "x", ring(NX, 1))
    back_a = lax.ppermute(given, "x", ring(NX, -1))
    fore_b = lax.ppermute((ahead + fore.astype(F32)).astype(BF16), "x", ring(NX, 1))
    back_b = lax.ppermute((behind + back.astype(F32)).astype(BF16), "x", ring(NX, -1))
    base = jnp.concatenate(
        [
            top + fore_b.astype(F32) + back_a.astype(F32),
            bottom + fore_a.astype(F32) + back_b.astype(F32),
        ],
        axis=0,
    )

    named = owner[:, 0]
    turn = jnp.arange(count, dtype=jnp.int32)
    earlier = (named[None, :] == named[:, None]) & (turn[None, :] < turn[:, None])
    position = jnp.sum(earlier.astype(jnp.int32), axis=1)
    place = (named % COLUMNS) * (NZ * CAP) + (named // COLUMNS) * CAP + position

    rows, base = lax.optimization_barrier((rows, base))
    part = down_step(order, rows, panels)
    parts = [part] + [lax.ppermute(part, "x", ring(NX, step)) for step in (1, 2, 3)]
    routes = ROUTES + ((0, 0),)
    y, core = lax.axis_index("y"), lax.axis_index("core")
    homes = jnp.stack([(y + dy) % NY * NC + (core + dc) % NC for dy, dc in routes])
    handlers = jnp.stack([(y - dy) % NY * NC + (core - dc) % NC for dy, dc in routes])
    pieces = up_step(order, homes, parts, panels, up.shape[2])
    pieces = [
        lax.ppermute(piece, GROUP, group_shift(*route)) for piece, route in zip(pieces, ROUTES)
    ] + [pieces[-1]]
    return final_step(handlers, place[:, None], pieces, base)


def solution(mesh):
    fine = Mesh(mesh.devices.reshape(NZ, NY, NC, NX), ("z", "y", "core", "x"))
    dp = ("z", "y", "core")
    placed = (P(dp, "x"), P(dp, None), P("x", None), P(dp, None, "x"), P(dp, None, "x"))
    return jax.shard_map(
        on_device, mesh=fine, in_specs=placed, out_specs=P(dp, "x"), check_vma=False
    )
```

```python
import jax
import jax.numpy as jnp
from jax import lax
from jax.experimental import pallas as pl
from jax.experimental.pallas import tpu as pltpu
from jax.sharding import Mesh, PartitionSpec as P

F32 = jnp.float32
BF16 = jnp.bfloat16
NZ, NY, NC, NX = 8, 4, 2, 4
COLUMNS = NY * NC
CAP = 16
GROUP = ("y", "core")
WHOLE, PART = 60, 16
ROUTES = ((2, 0), (2, 1), (1, 0), (3, 0), (1, 1), (3, 1), (0, 1))
RELATIVE_Z = (0, -1, 1, -2, 2, -3, 3, -4)
ORDER, HOMES, HANDLERS = 4, 12, 20


def ring(size, step):
    return [(place, (place + step) % size) for place in range(size)]


def call(kernel, name, out, grid, ins, outs, flops, moved, limit, prefetch=0, scratch=()):
    return pl.pallas_call(
        kernel,
        out_shape=out,
        grid_spec=pltpu.PrefetchScalarGridSpec(
            num_scalar_prefetch=prefetch,
            grid=grid,
            in_specs=ins,
            out_specs=outs,
            scratch_shapes=scratch,
        ),
        compiler_params=pltpu.CompilerParams(vmem_limit_bytes=limit * 1024 * 1024),
        cost_estimate=pl.CostEstimate(flops=flops, bytes_accessed=moved, transcendentals=0),
        name=name,
    )


def base_kernel(table, tokens, weight, *outs):
    product = jnp.dot(tokens[...], weight[...], preferred_element_type=F32)
    half = product.shape[0] // 2
    for j in range(2):

        @pl.when(pl.program_id(0) == j)
        def _():
            top, bottom = outs[2 * j : 2 * j + 2]
            top[...] = product[:half].astype(top.dtype)
            bottom[...] = product[half:].astype(bottom.dtype)


def base_pair(tokens, weight, table, start, types, tile=256):
    count, inner = tokens.shape
    width = weight.shape[1] // NX
    tiles = width // tile
    first = pl.BlockSpec((count // 2, tile), lambda j, n, w: (0, n + j * (tiles - 1 - n)))
    second = pl.BlockSpec((count // 2, tile), lambda j, n, w: (0, n * j))
    return call(
        base_kernel,
        "base",
        [jax.ShapeDtypeStruct((count // 2, width), kind) for kind in types],
        (2, tiles),
        [
            pl.BlockSpec((count, inner), lambda j, n, w: (0, 0)),
            pl.BlockSpec((inner, tile), lambda j, n, w: (0, w[start + j] * tiles + n)),
        ],
        [first, first, second, second],
        4 * count * inner * width,
        2 * (count + 2 * width) * inner,
        WHOLE,
        prefetch=1,
    )(table, tokens, weight)


def dispatch_kernel(owner, tokens, out, chosen, held, made, taken, given):
    count = held.shape[0]
    slots = chosen.shape[0]
    width = held.shape[1] // taken.shape[0]
    blocks = [pl.ds(part * width, width) for part in range(taken.shape[0])]
    fetches = [
        pltpu.make_async_copy(tokens.at[:, block], held.at[:, block], taken.at[part])
        for part, block in enumerate(blocks)
    ]
    for fetch in fetches:
        fetch.start()
    mine = owner[...]
    adapter = lax.broadcasted_iota(jnp.int32, (NZ * COLUMNS, count), 0)
    member = (adapter == mine).astype(F32)
    above = lax.broadcasted_iota(jnp.int32, (count, count), 0)
    below = lax.broadcasted_iota(jnp.int32, (count, count), 1)
    before = (above < below).astype(F32).astype(BF16)
    earlier = jnp.dot(member.astype(BF16), before, preferred_element_type=F32)
    position = jnp.sum(earlier * member, axis=0, keepdims=True).astype(jnp.int32)
    place = (mine % COLUMNS) * (NZ * CAP) + (mine // COLUMNS) * CAP + position
    slot = lax.broadcasted_iota(jnp.int32, (slots, count), 0)
    chosen[...] = (slot == place).astype(F32).astype(BF16)
    copies = []
    for part, block in enumerate(blocks):
        fetches[part].wait()
        product = jnp.dot(chosen[...], held[:, block], preferred_element_type=F32)
        made[:, :, block] = product.astype(BF16).reshape(made.shape[0], made.shape[1], width)
        copy = pltpu.make_async_copy(made.at[:, :, block], out.at[:, :, block], given.at[part])
        copy.start()
        copies.append(copy)
    for copy in copies:
        copy.wait()


def dispatch(tokens, owner):
    count, inner = tokens.shape
    rows = NZ * CAP
    whole = pl.BlockSpec(memory_space=pl.ANY)
    return call(
        dispatch_kernel,
        "dispatch",
        jax.ShapeDtypeStruct((COLUMNS, rows, inner), BF16),
        (1,),
        [pl.BlockSpec((1, count), lambda n: (0, 0)), whole],
        whole,
        2 * COLUMNS * rows * count * inner,
        2 * (count + COLUMNS * rows) * inner,
        WHOLE,
        scratch=[
            pltpu.VMEM((COLUMNS * rows, count), BF16),
            pltpu.VMEM((count, inner), BF16),
            pltpu.VMEM((COLUMNS, rows, inner), BF16),
            pltpu.SemaphoreType.DMA((4,)),
            pltpu.SemaphoreType.DMA((4,)),
        ],
    )(owner.reshape(1, count), tokens)


def down_kernel(table, rows, *refs):
    panels, (out, held, kept, first, second) = refs[:NZ], refs[NZ:]
    inner = rows.shape[2]
    copies = []
    for i in range(NZ):
        start = pl.multiple_of(table[ORDER + i] * CAP, CAP)
        pair = (
            pltpu.make_async_copy(rows.at[:, pl.ds(start, CAP), :], held.at[i], first.at[i]),
            pltpu.make_async_copy(panels[i].at[:, pl.ds(0, inner)], kept.at[i], second.at[i]),
        )
        for copy in pair:
            copy.start()
        copies.append(pair)
    many, rank = 4, kept.shape[1]
    lines = COLUMNS * CAP
    for start in range(0, NZ, many):
        for pair in copies[start : start + many]:
            for copy in pair:
                copy.wait()
        product = lax.dot_general(
            kept[start : start + many].reshape(many * rank, inner),
            held[start : start + many].reshape(many * lines, inner),
            (((1,), (1,)), ((), ())),
            preferred_element_type=F32,
        )
        for i in range(many):
            block = product[i * rank : (i + 1) * rank, i * lines : (i + 1) * lines]
            out[start + i] = block.astype(BF16)


def down_step(table, rows, panels):
    inner = rows.shape[2]
    rank = panels[0].shape[0]
    lines = COLUMNS * CAP
    whole = pl.BlockSpec(memory_space=pl.ANY)
    return call(
        down_kernel,
        "down",
        jax.ShapeDtypeStruct((NZ, rank, lines), BF16),
        (1,),
        [whole] * (1 + NZ),
        pl.BlockSpec(memory_space=pltpu.VMEM),
        2 * NZ * lines * inner * rank,
        2 * NZ * (lines + rank) * inner,
        PART,
        prefetch=1,
        scratch=[
            pltpu.VMEM((NZ, COLUMNS, CAP, inner), BF16),
            pltpu.VMEM((NZ, rank, inner), BF16),
            pltpu.SemaphoreType.DMA((NZ,)),
            pltpu.SemaphoreType.DMA((NZ,)),
        ],
    )(table, rows, *panels)


def collect_kernel(*refs):
    panels, (out, arrived) = refs[:NZ], refs[NZ:]
    width = out.shape[2]
    copies = [
        pltpu.make_async_copy(
            panels[i].at[:, pl.ds(panels[i].shape[1] - width, width)], out.at[i], arrived.at[i]
        )
        for i in range(NZ)
    ]
    for copy in copies:
        copy.start()
    for copy in copies:
        copy.wait()


def collect(panels, width):
    rank = panels[0].shape[0]
    return call(
        collect_kernel,
        "collect",
        jax.ShapeDtypeStruct((NZ, rank, width), BF16),
        (1,),
        [pl.BlockSpec(memory_space=pl.ANY)] * NZ,
        pl.BlockSpec(memory_space=pltpu.VMEM),
        0,
        4 * NZ * rank * width,
        PART,
        scratch=[pltpu.SemaphoreType.DMA((NZ,))],
    )(*panels)


def up_kernel(table, *refs):
    parts, panels, outs, low = refs[:NX], refs[NX], refs[NX + 1 : -1], refs[-1]
    for i in range(NZ):
        total = parts[0][i].astype(F32)
        for part in parts[1:]:
            total = total + part[i].astype(F32)
        low[i] = total.T
        picked = [
            low[i, pl.ds(pl.multiple_of(table[HOMES + r] * CAP, CAP), CAP), :]
            for r in range(COLUMNS)
        ]
        delta = jnp.dot(
            jnp.concatenate(picked, axis=0).astype(BF16), panels[i], preferred_element_type=F32
        ).astype(BF16)
        start = pl.multiple_of(table[ORDER + i] * CAP, CAP)
        for r in range(COLUMNS):
            outs[r][pl.ds(start, CAP), :] = delta[r * CAP : (r + 1) * CAP]


def up_step(table, parts, panels):
    _, rank, width = panels.shape
    lines = COLUMNS * CAP
    near = pl.BlockSpec(memory_space=pltpu.VMEM)
    return call(
        up_kernel,
        "up",
        [jax.ShapeDtypeStruct((NZ * CAP, width), BF16)] * COLUMNS,
        (1,),
        [near] * (NX + 1),
        [near] * COLUMNS,
        2 * NZ * lines * rank * width,
        2 * NZ * (lines + rank) * width,
        PART,
        prefetch=1,
        scratch=[pltpu.VMEM((NZ, lines, rank), F32)],
    )(table, *parts, panels)


def final_kernel(table, place, base, *refs):
    pieces, (out, held, made, taken, sent) = refs[:COLUMNS], refs[COLUMNS:]
    fetch = pltpu.make_async_copy(pieces[-1], held, taken)
    fetch.start()
    rows, width = pieces[0].shape
    count = made.shape[0]
    turn = lax.broadcasted_iota(jnp.int32, (count, rows), 1)
    named = place[...]
    chosen = jnp.concatenate(
        [
            (turn + table[HANDLERS + r] * rows == named).astype(F32).astype(BF16)
            for r in range(COLUMNS)
        ],
        axis=1,
    )
    fetch.wait()
    delta = jnp.concatenate([piece[...] for piece in pieces[:-1]] + [held[...]], axis=0)
    copies = []
    parts = sent.shape[0]
    tall = count // parts
    for part in range(parts):
        some = pl.ds(part * tall, tall)
        mine = jnp.dot(
            chosen[part * tall : (part + 1) * tall], delta, preferred_element_type=F32
        )
        made[some] = (base[some] + mine).astype(made.dtype)
        copy = pltpu.make_async_copy(made.at[some], out.at[some], sent.at[part])
        copy.start()
        copies.append(copy)
    for copy in copies:
        copy.wait()


def final_step(table, place, pieces, base):
    count = place.shape[0]
    rows, width = pieces[0].shape
    slots = COLUMNS * rows
    near = pl.BlockSpec(memory_space=pltpu.VMEM)
    return call(
        final_kernel,
        "final",
        jax.ShapeDtypeStruct((count, width), BF16),
        (1,),
        [pl.BlockSpec((count, 1), lambda n, t: (0, 0))] + [near] * COLUMNS + [pl.BlockSpec(memory_space=pltpu.HBM)],
        pl.BlockSpec(memory_space=pltpu.HBM),
        2 * count * slots * width,
        2 * (slots + 4 * count) * width,
        PART,
        prefetch=1,
        scratch=[
            pltpu.VMEM((rows, width), BF16),
            pltpu.VMEM((count, width), BF16),
            pltpu.SemaphoreType.DMA,
            pltpu.SemaphoreType.DMA((2,)),
        ],
    )(table, place, base, *pieces)


def group_shift(dy, dc):
    return [
        (y * NC + core, (y + dy) % NY * NC + (core + dc) % NC)
        for y in range(NY)
        for core in range(NC)
    ]


def z_ring(chunk):
    fore = back = chunk
    found = [chunk]
    for step in range(1, 5):
        fore = lax.ppermute(fore, "z", ring(NZ, 1))
        found.append(fore)
        if step < 4:
            back = lax.ppermute(back, "z", ring(NZ, -1))
            found.append(back)
    return found


def on_device(tokens, owner, weight, down, up):
    z, y, core, x = (lax.axis_index(name) for name in ("z", "y", "core", "x"))
    count = tokens.shape[0]
    routes = ROUTES + ((0, 0),)
    table = jnp.stack(
        [(x + 2) % NX, (x + 1) % NX, (x + 3) % NX, x]
        + [(z + dz) % NZ for dz in RELATIVE_Z]
        + [(y + dy) % NY * NC + (core + dc) % NC for dy, dc in routes]
        + [(y - dy) % NY * NC + (core - dc) % NC for dy, dc in routes]
    )

    rows = lax.all_to_all(dispatch(tokens, owner), GROUP, 0, 0, tiled=True)
    panels = z_ring(jnp.concatenate([down[0], up[0]], axis=1))

    fore, back, ahead, sent = base_pair(tokens, weight, table, 0, (BF16, BF16, F32, BF16))
    tokens, fore = lax.optimization_barrier((tokens, fore))
    given, behind, top, bottom = base_pair(tokens, weight, table, 2, (BF16, F32, F32, F32))
    fore = lax.ppermute(fore, "x", ring(NX, 1))
    back = lax.ppermute(back, "x", ring(NX, -1))
    fore_a = lax.ppermute(sent, "x", ring(NX, 1))
    back_a = lax.ppermute(given, "x", ring(NX, -1))
    fore_b = lax.ppermute((ahead + fore.astype(F32)).astype(BF16), "x", ring(NX, 1))
    back_b = lax.ppermute((behind + back.astype(F32)).astype(BF16), "x", ring(NX, -1))
    base = jnp.concatenate(
        [
            top + fore_b.astype(F32) + back_a.astype(F32),
            bottom + fore_a.astype(F32) + back_b.astype(F32),
        ],
        axis=0,
    )

    named = owner[:, 0]
    turn = jnp.arange(count, dtype=jnp.int32)
    earlier = (named[None, :] == named[:, None]) & (turn[None, :] < turn[:, None])
    position = jnp.sum(earlier.astype(jnp.int32), axis=1)
    place = (named % COLUMNS) * (NZ * CAP) + (named // COLUMNS) * CAP + position

    rows, base = lax.optimization_barrier((rows, base))
    part = down_step(table, rows, panels)
    parts = [part] + [lax.ppermute(part, "x", ring(NX, step)) for step in (1, 2, 3)]
    pieces = up_step(table, parts, collect(panels, up.shape[2]))
    pieces = [
        lax.ppermute(piece, GROUP, group_shift(*route)) for piece, route in zip(pieces, ROUTES)
    ] + [pieces[-1]]
    return final_step(table, place[:, None], pieces, base)


def solution(mesh):
    fine = Mesh(mesh.devices.reshape(NZ, NY, NC, NX), ("z", "y", "core", "x"))
    dp = ("z", "y", "core")
    placed = (P(dp, "x"), P(dp, None), P("x", None), P(dp, None, "x"), P(dp, None, "x"))
    return jax.shard_map(
        on_device, mesh=fine, in_specs=placed, out_specs=P(dp, "x"), check_vma=False
    )
```

```python
import functools

import jax
import jax.numpy as jnp
from jax import lax
from jax.experimental import pallas as pl
from jax.experimental.pallas import tpu as pltpu
from jax.sharding import Mesh, PartitionSpec as P

F32 = jnp.float32
BF16 = jnp.bfloat16
NZ, NY, NC, NX = 8, 4, 2, 4
COLUMNS = NY * NC
CAP = 16
EARLY = 5
GROUP = ("y", "core")
WHOLE, PART = 60, 16
ROUTES = ((2, 0), (2, 1), (1, 0), (3, 0), (1, 1), (3, 1), (0, 1))
RELATIVE_Z = (0, -1, 1, -2, 2, -3, 3, -4)
ORDER, HOMES, HANDLERS = 4, 12, 20


def ring(size, step):
    return [(place, (place + step) % size) for place in range(size)]


def call(kernel, name, out, grid, ins, outs, flops, moved, limit, prefetch=0, scratch=()):
    return pl.pallas_call(
        kernel,
        out_shape=out,
        grid_spec=pltpu.PrefetchScalarGridSpec(
            num_scalar_prefetch=prefetch,
            grid=grid,
            in_specs=ins,
            out_specs=outs,
            scratch_shapes=scratch,
        ),
        compiler_params=pltpu.CompilerParams(vmem_limit_bytes=limit * 1024 * 1024),
        cost_estimate=pl.CostEstimate(flops=flops, bytes_accessed=moved, transcendentals=0),
        name=name,
    )


def base_kernel(table, tokens, weight, *outs):
    product = jnp.dot(tokens[...], weight[...], preferred_element_type=F32)
    half = product.shape[0] // 2
    for j in range(2):

        @pl.when(pl.program_id(0) == j)
        def _():
            top, bottom = outs[2 * j : 2 * j + 2]
            top[...] = product[:half].astype(top.dtype)
            bottom[...] = product[half:].astype(bottom.dtype)


def base_pair(tokens, weight, table, start, types, tile=256):
    count, inner = tokens.shape
    width = weight.shape[1] // NX
    tiles = width // tile
    first = pl.BlockSpec((count // 2, tile), lambda j, n, w: (0, n + j * (tiles - 1 - n)))
    second = pl.BlockSpec((count // 2, tile), lambda j, n, w: (0, n * j))
    return call(
        base_kernel,
        "base",
        [jax.ShapeDtypeStruct((count // 2, width), kind) for kind in types],
        (2, tiles),
        [
            pl.BlockSpec((count, inner), lambda j, n, w: (0, 0)),
            pl.BlockSpec((inner, tile), lambda j, n, w: (0, w[start + j] * tiles + n)),
        ],
        [first, first, second, second],
        4 * count * inner * width,
        2 * (count + 2 * width) * inner,
        WHOLE,
        prefetch=1,
    )(table, tokens, weight)


def dispatch_kernel(owner, tokens, out, chosen, held, made, taken, given):
    count = held.shape[0]
    slots = chosen.shape[0]
    width = held.shape[1] // taken.shape[0]
    blocks = [pl.ds(part * width, width) for part in range(taken.shape[0])]
    fetches = [
        pltpu.make_async_copy(tokens.at[:, block], held.at[:, block], taken.at[part])
        for part, block in enumerate(blocks)
    ]
    for fetch in fetches:
        fetch.start()
    mine = owner[...]
    adapter = lax.broadcasted_iota(jnp.int32, (NZ * COLUMNS, count), 0)
    member = (adapter == mine).astype(F32)
    above = lax.broadcasted_iota(jnp.int32, (count, count), 0)
    below = lax.broadcasted_iota(jnp.int32, (count, count), 1)
    before = (above < below).astype(F32).astype(BF16)
    earlier = jnp.dot(member.astype(BF16), before, preferred_element_type=F32)
    position = jnp.sum(earlier * member, axis=0, keepdims=True).astype(jnp.int32)
    place = (mine % COLUMNS) * (NZ * CAP) + (mine // COLUMNS) * CAP + position
    slot = lax.broadcasted_iota(jnp.int32, (slots, count), 0)
    chosen[...] = (slot == place).astype(F32).astype(BF16)
    copies = []
    for part, block in enumerate(blocks):
        fetches[part].wait()
        product = jnp.dot(chosen[...], held[:, block], preferred_element_type=F32)
        made[:, :, block] = product.astype(BF16).reshape(made.shape[0], made.shape[1], width)
        copy = pltpu.make_async_copy(made.at[:, :, block], out.at[:, :, block], given.at[part])
        copy.start()
        copies.append(copy)
    for copy in copies:
        copy.wait()


def dispatch(tokens, owner):
    count, inner = tokens.shape
    rows = NZ * CAP
    whole = pl.BlockSpec(memory_space=pl.ANY)
    return call(
        dispatch_kernel,
        "dispatch",
        jax.ShapeDtypeStruct((COLUMNS, rows, inner), BF16),
        (1,),
        [pl.BlockSpec((1, count), lambda n: (0, 0)), whole],
        whole,
        2 * COLUMNS * rows * count * inner,
        2 * (count + COLUMNS * rows) * inner,
        WHOLE,
        scratch=[
            pltpu.VMEM((COLUMNS * rows, count), BF16),
            pltpu.VMEM((count, inner), BF16),
            pltpu.VMEM((COLUMNS, rows, inner), BF16),
            pltpu.SemaphoreType.DMA((4,)),
            pltpu.SemaphoreType.DMA((4,)),
        ],
    )(owner.reshape(1, count), tokens)


def down_kernel(table, rows, *refs):
    panels, (out, held, kept, first, second) = refs[:NZ], refs[NZ:]
    inner = rows.shape[2]
    copies = []
    for i in range(NZ):
        start = pl.multiple_of(table[ORDER + i] * CAP, CAP)
        pair = (
            pltpu.make_async_copy(rows.at[:, pl.ds(start, CAP), :], held.at[i], first.at[i]),
            pltpu.make_async_copy(panels[i].at[:, pl.ds(0, inner)], kept.at[i], second.at[i]),
        )
        for copy in pair:
            copy.start()
        copies.append(pair)
    many, rank = 4, kept.shape[1]
    lines = COLUMNS * CAP
    for start in range(0, NZ, many):
        for pair in copies[start : start + many]:
            for copy in pair:
                copy.wait()
        product = lax.dot_general(
            kept[start : start + many].reshape(many * rank, inner),
            held[start : start + many].reshape(many * lines, inner),
            (((1,), (1,)), ((), ())),
            preferred_element_type=F32,
        )
        for i in range(many):
            block = product[i * rank : (i + 1) * rank, i * lines : (i + 1) * lines]
            out[start + i] = block.astype(BF16)


def down_step(table, rows, panels):
    inner = rows.shape[2]
    rank = panels[0].shape[0]
    lines = COLUMNS * CAP
    whole = pl.BlockSpec(memory_space=pl.ANY)
    return call(
        down_kernel,
        "down",
        jax.ShapeDtypeStruct((NZ, rank, lines), BF16),
        (1,),
        [whole] * (1 + NZ),
        pl.BlockSpec(memory_space=pltpu.VMEM),
        2 * NZ * lines * inner * rank,
        2 * NZ * (lines + rank) * inner,
        PART,
        prefetch=1,
        scratch=[
            pltpu.VMEM((NZ, COLUMNS, CAP, inner), BF16),
            pltpu.VMEM((NZ, rank, inner), BF16),
            pltpu.SemaphoreType.DMA((NZ,)),
            pltpu.SemaphoreType.DMA((NZ,)),
        ],
    )(table, rows, *panels)


def collect_kernel(*refs):
    panels, (out, arrived) = refs[:NZ], refs[NZ:]
    width = out.shape[2]
    copies = [
        pltpu.make_async_copy(
            panels[i].at[:, pl.ds(panels[i].shape[1] - width, width)], out.at[i], arrived.at[i]
        )
        for i in range(NZ)
    ]
    for copy in copies:
        copy.start()
    for copy in copies:
        copy.wait()


def collect(panels, width):
    rank = panels[0].shape[0]
    return call(
        collect_kernel,
        "collect",
        jax.ShapeDtypeStruct((NZ, rank, width), BF16),
        (1,),
        [pl.BlockSpec(memory_space=pl.ANY)] * NZ,
        pl.BlockSpec(memory_space=pltpu.VMEM),
        0,
        4 * NZ * rank * width,
        PART,
        scratch=[pltpu.SemaphoreType.DMA((NZ,))],
    )(*panels)


def up_kernel(table, *refs):
    parts, panels, outs, low = refs[:NX], refs[NX], refs[NX + 1 : -1], refs[-1]
    for i in range(NZ):
        total = parts[0][i].astype(F32)
        for part in parts[1:]:
            total = total + part[i].astype(F32)
        low[i] = total.T
        picked = [
            low[i, pl.ds(pl.multiple_of(table[HOMES + r] * CAP, CAP), CAP), :]
            for r in range(COLUMNS)
        ]
        delta = jnp.dot(
            jnp.concatenate(picked, axis=0).astype(BF16), panels[i], preferred_element_type=F32
        ).astype(BF16)
        start = pl.multiple_of(table[ORDER + i] * CAP, CAP)
        for r in range(COLUMNS):
            outs[r][pl.ds(start, CAP), :] = delta[r * CAP : (r + 1) * CAP]


def up_step(table, parts, panels):
    _, rank, width = panels.shape
    lines = COLUMNS * CAP
    near = pl.BlockSpec(memory_space=pltpu.VMEM)
    return call(
        up_kernel,
        "up",
        [jax.ShapeDtypeStruct((NZ * CAP, width), BF16)] * COLUMNS,
        (1,),
        [near] * (NX + 1),
        [near] * COLUMNS,
        2 * NZ * lines * rank * width,
        2 * NZ * (lines + rank) * width,
        PART,
        prefetch=1,
        scratch=[pltpu.VMEM((NZ, lines, rank), F32)],
    )(table, *parts, panels)


def place_pieces(table, start, named, pieces):
    rows = pieces[0].shape[0]
    turn = lax.broadcasted_iota(jnp.int32, (named.shape[0], rows), 1)
    chosen = jnp.concatenate(
        [
            (turn + table[HANDLERS + start + r] * rows == named).astype(F32).astype(BF16)
            for r in range(len(pieces))
        ],
        axis=1,
    )
    delta = jnp.concatenate([piece[...] for piece in pieces], axis=0)
    return jnp.dot(chosen, delta, preferred_element_type=F32)


def early_kernel(start, table, place, base, *refs):
    pieces, out = refs[:-1], refs[-1]
    out[...] = base[...] + place_pieces(table, start, place[...], pieces)


def early_step(table, start, place, pieces, base):
    count = place.shape[0]
    rows, width = pieces[0].shape
    near = pl.BlockSpec(memory_space=pltpu.VMEM)
    return call(
        functools.partial(early_kernel, start),
        "early",
        jax.ShapeDtypeStruct((count, width), F32),
        (1,),
        [pl.BlockSpec((count, 1), lambda n, t: (0, 0))] + [near] * (1 + len(pieces)),
        near,
        2 * count * rows * len(pieces) * width,
        4 * count * width,
        PART,
        prefetch=1,
    )(table, place, base, *pieces)


def final_kernel(start, table, place, base, *refs):
    pieces, (out, made, sent) = refs[:-3], refs[-3:]
    count = made.shape[0]
    copies = []
    parts = sent.shape[0]
    tall = count // parts
    for part in range(parts):
        some = pl.ds(part * tall, tall)
        mine = place_pieces(table, start, place[some], pieces)
        made[some] = (base[some] + mine).astype(made.dtype)
        copy = pltpu.make_async_copy(made.at[some], out.at[some], sent.at[part])
        copy.start()
        copies.append(copy)
    for copy in copies:
        copy.wait()


def final_step(table, start, place, pieces, base):
    count = place.shape[0]
    rows, width = pieces[0].shape
    near = pl.BlockSpec(memory_space=pltpu.VMEM)
    return call(
        functools.partial(final_kernel, start),
        "final",
        jax.ShapeDtypeStruct((count, width), BF16),
        (1,),
        [near] * (2 + len(pieces)),
        pl.BlockSpec(memory_space=pltpu.HBM),
        2 * count * rows * len(pieces) * width,
        4 * count * width,
        PART,
        prefetch=1,
        scratch=[pltpu.VMEM((count, width), BF16), pltpu.SemaphoreType.DMA((2,))],
    )(table, place, base, *pieces)


def group_shift(dy, dc):
    return [
        (y * NC + core, (y + dy) % NY * NC + (core + dc) % NC)
        for y in range(NY)
        for core in range(NC)
    ]


def z_ring(chunk):
    fore = back = chunk
    found = [chunk]
    for step in range(1, 5):
        fore = lax.ppermute(fore, "z", ring(NZ, 1))
        found.append(fore)
        if step < 4:
            back = lax.ppermute(back, "z", ring(NZ, -1))
            found.append(back)
    return found


def on_device(tokens, owner, weight, down, up):
    z, y, core, x = (lax.axis_index(name) for name in ("z", "y", "core", "x"))
    count = tokens.shape[0]
    routes = ((0, 0),) + ROUTES
    table = jnp.stack(
        [(x + 2) % NX, (x + 1) % NX, (x + 3) % NX, x]
        + [(z + dz) % NZ for dz in RELATIVE_Z]
        + [(y + dy) % NY * NC + (core + dc) % NC for dy, dc in routes]
        + [(y - dy) % NY * NC + (core - dc) % NC for dy, dc in routes]
    )

    rows = lax.all_to_all(dispatch(tokens, owner), GROUP, 0, 0, tiled=True)
    panels = z_ring(jnp.concatenate([down[0], up[0]], axis=1))

    fore, back, ahead, sent = base_pair(tokens, weight, table, 0, (BF16, BF16, F32, BF16))
    tokens, fore = lax.optimization_barrier((tokens, fore))
    given, behind, top, bottom = base_pair(tokens, weight, table, 2, (BF16, F32, F32, F32))
    fore = lax.ppermute(fore, "x", ring(NX, 1))
    back = lax.ppermute(back, "x", ring(NX, -1))
    fore_a = lax.ppermute(sent, "x", ring(NX, 1))
    back_a = lax.ppermute(given, "x", ring(NX, -1))
    fore_b = lax.ppermute((ahead + fore.astype(F32)).astype(BF16), "x", ring(NX, 1))
    back_b = lax.ppermute((behind + back.astype(F32)).astype(BF16), "x", ring(NX, -1))
    base = jnp.concatenate(
        [
            top + fore_b.astype(F32) + back_a.astype(F32),
            bottom + fore_a.astype(F32) + back_b.astype(F32),
        ],
        axis=0,
    )

    named = owner[:, 0]
    turn = jnp.arange(count, dtype=jnp.int32)
    earlier = (named[None, :] == named[:, None]) & (turn[None, :] < turn[:, None])
    position = jnp.sum(earlier.astype(jnp.int32), axis=1)
    place = (named % COLUMNS) * (NZ * CAP) + (named // COLUMNS) * CAP + position

    rows, base = lax.optimization_barrier((rows, base))
    part = down_step(table, rows, panels)
    parts = [part] + [lax.ppermute(part, "x", ring(NX, step)) for step in (2, 1, 3)]
    pieces = up_step(table, parts, collect(panels, up.shape[2]))
    pieces = [pieces[0]] + [
        lax.ppermute(piece, GROUP, group_shift(*route)) for piece, route in zip(pieces[1:], ROUTES)
    ]
    place = place[:, None]
    base = early_step(table, 0, place, pieces[:EARLY], base)
    return final_step(table, EARLY, place, pieces[EARLY:], base)


def solution(mesh):
    fine = Mesh(mesh.devices.reshape(NZ, NY, NC, NX), ("z", "y", "core", "x"))
    dp = ("z", "y", "core")
    placed = (P(dp, "x"), P(dp, None), P("x", None), P(dp, None, "x"), P(dp, None, "x"))
    return jax.shard_map(
        on_device, mesh=fine, in_specs=placed, out_specs=P(dp, "x"), check_vma=False
    )
```

```python
import functools

import jax
import jax.numpy as jnp
from jax import lax
from jax.experimental import pallas as pl
from jax.experimental.pallas import tpu as pltpu
from jax.sharding import Mesh, PartitionSpec as P

F32 = jnp.float32
BF16 = jnp.bfloat16
NZ, NY, NC, NX = 8, 4, 2, 4
COLUMNS = NY * NC
CAP = 16
EARLY = 6
GROUP = ("y", "core")
WHOLE, PART = 60, 16
ROUTES = ((2, 0), (2, 1), (1, 0), (3, 0), (0, 1), (1, 1), (3, 1))
RELATIVE_Z = (0, -1, 1, -2, 2, -3, 3, -4)
ORDER, HOMES, HANDLERS = 4, 12, 20


def ring(size, step):
    return [(place, (place + step) % size) for place in range(size)]


def call(kernel, name, out, grid, ins, outs, flops, moved, limit, prefetch=0, scratch=()):
    return pl.pallas_call(
        kernel,
        out_shape=out,
        grid_spec=pltpu.PrefetchScalarGridSpec(
            num_scalar_prefetch=prefetch,
            grid=grid,
            in_specs=ins,
            out_specs=outs,
            scratch_shapes=scratch,
        ),
        compiler_params=pltpu.CompilerParams(vmem_limit_bytes=limit * 1024 * 1024),
        cost_estimate=pl.CostEstimate(flops=flops, bytes_accessed=moved, transcendentals=0),
        name=name,
    )


def base_kernel(table, tokens, weight, *outs):
    product = jnp.dot(tokens[...], weight[...], preferred_element_type=F32)
    half = product.shape[0] // 2
    for j in range(2):

        @pl.when(pl.program_id(0) == j)
        def _():
            top, bottom = outs[2 * j : 2 * j + 2]
            top[...] = product[:half].astype(top.dtype)
            bottom[...] = product[half:].astype(bottom.dtype)


def base_pair(tokens, weight, table, start, types, tile=256):
    count, inner = tokens.shape
    width = weight.shape[1] // NX
    tiles = width // tile
    first = pl.BlockSpec((count // 2, tile), lambda j, n, w: (0, n + j * (tiles - 1 - n)))
    second = pl.BlockSpec((count // 2, tile), lambda j, n, w: (0, n * j))
    return call(
        base_kernel,
        "base",
        [jax.ShapeDtypeStruct((count // 2, width), kind) for kind in types],
        (2, tiles),
        [
            pl.BlockSpec((count, inner), lambda j, n, w: (0, 0)),
            pl.BlockSpec((inner, tile), lambda j, n, w: (0, w[start + j] * tiles + n)),
        ],
        [first, first, second, second],
        4 * count * inner * width,
        2 * (count + 2 * width) * inner,
        WHOLE,
        prefetch=1,
    )(table, tokens, weight)


def dispatch_kernel(owner, tokens, out, chosen, held, made, taken, given):
    count = held.shape[0]
    slots = chosen.shape[0]
    width = held.shape[1] // taken.shape[0]
    blocks = [pl.ds(part * width, width) for part in range(taken.shape[0])]
    fetches = [
        pltpu.make_async_copy(tokens.at[:, block], held.at[:, block], taken.at[part])
        for part, block in enumerate(blocks)
    ]
    for fetch in fetches:
        fetch.start()
    mine = owner[...]
    adapter = lax.broadcasted_iota(jnp.int32, (NZ * COLUMNS, count), 0)
    member = (adapter == mine).astype(F32)
    above = lax.broadcasted_iota(jnp.int32, (count, count), 0)
    below = lax.broadcasted_iota(jnp.int32, (count, count), 1)
    before = (above < below).astype(F32).astype(BF16)
    earlier = jnp.dot(member.astype(BF16), before, preferred_element_type=F32)
    position = jnp.sum(earlier * member, axis=0, keepdims=True).astype(jnp.int32)
    place = (mine % COLUMNS) * (NZ * CAP) + (mine // COLUMNS) * CAP + position
    slot = lax.broadcasted_iota(jnp.int32, (slots, count), 0)
    chosen[...] = (slot == place).astype(F32).astype(BF16)
    copies = []
    for part, block in enumerate(blocks):
        fetches[part].wait()
        product = jnp.dot(chosen[...], held[:, block], preferred_element_type=F32)
        made[:, :, block] = product.astype(BF16).reshape(made.shape[0], made.shape[1], width)
        copy = pltpu.make_async_copy(made.at[:, :, block], out.at[:, :, block], given.at[part])
        copy.start()
        copies.append(copy)
    for copy in copies:
        copy.wait()


def dispatch(tokens, owner):
    count, inner = tokens.shape
    rows = NZ * CAP
    whole = pl.BlockSpec(memory_space=pl.ANY)
    return call(
        dispatch_kernel,
        "dispatch",
        jax.ShapeDtypeStruct((COLUMNS, rows, inner), BF16),
        (1,),
        [pl.BlockSpec((1, count), lambda n: (0, 0)), whole],
        whole,
        2 * COLUMNS * rows * count * inner,
        2 * (count + COLUMNS * rows) * inner,
        WHOLE,
        scratch=[
            pltpu.VMEM((COLUMNS * rows, count), BF16),
            pltpu.VMEM((count, inner), BF16),
            pltpu.VMEM((COLUMNS, rows, inner), BF16),
            pltpu.SemaphoreType.DMA((4,)),
            pltpu.SemaphoreType.DMA((4,)),
        ],
    )(owner.reshape(1, count), tokens)


def down_kernel(table, rows, *refs):
    panels, (out, held, kept, first, second) = refs[:NZ], refs[NZ:]
    inner = rows.shape[2]
    copies = []
    for i in range(NZ):
        start = pl.multiple_of(table[ORDER + i] * CAP, CAP)
        pair = (
            pltpu.make_async_copy(rows.at[:, pl.ds(start, CAP), :], held.at[i], first.at[i]),
            pltpu.make_async_copy(panels[i].at[:, pl.ds(0, inner)], kept.at[i], second.at[i]),
        )
        for copy in pair:
            copy.start()
        copies.append(pair)
    many, rank = 4, kept.shape[1]
    lines = COLUMNS * CAP
    for start in range(0, NZ, many):
        for pair in copies[start : start + many]:
            for copy in pair:
                copy.wait()
        product = lax.dot_general(
            kept[start : start + many].reshape(many * rank, inner),
            held[start : start + many].reshape(many * lines, inner),
            (((1,), (1,)), ((), ())),
            preferred_element_type=F32,
        )
        for i in range(many):
            block = product[i * rank : (i + 1) * rank, i * lines : (i + 1) * lines]
            out[start + i] = block.astype(BF16)


def down_step(table, rows, panels):
    inner = rows.shape[2]
    rank = panels[0].shape[0]
    lines = COLUMNS * CAP
    whole = pl.BlockSpec(memory_space=pl.ANY)
    return call(
        down_kernel,
        "down",
        jax.ShapeDtypeStruct((NZ, rank, lines), BF16),
        (1,),
        [whole] * (1 + NZ),
        pl.BlockSpec(memory_space=pltpu.VMEM),
        2 * NZ * lines * inner * rank,
        2 * NZ * (lines + rank) * inner,
        PART,
        prefetch=1,
        scratch=[
            pltpu.VMEM((NZ, COLUMNS, CAP, inner), BF16),
            pltpu.VMEM((NZ, rank, inner), BF16),
            pltpu.SemaphoreType.DMA((NZ,)),
            pltpu.SemaphoreType.DMA((NZ,)),
        ],
    )(table, rows, *panels)


def collect_kernel(*refs):
    panels, (out, arrived) = refs[:NZ], refs[NZ:]
    width = out.shape[2]
    copies = [
        pltpu.make_async_copy(
            panels[i].at[:, pl.ds(panels[i].shape[1] - width, width)], out.at[i], arrived.at[i]
        )
        for i in range(NZ)
    ]
    for copy in copies:
        copy.start()
    for copy in copies:
        copy.wait()


def collect(panels, width):
    rank = panels[0].shape[0]
    return call(
        collect_kernel,
        "collect",
        jax.ShapeDtypeStruct((NZ, rank, width), BF16),
        (1,),
        [pl.BlockSpec(memory_space=pl.ANY)] * NZ,
        pl.BlockSpec(memory_space=pltpu.VMEM),
        0,
        4 * NZ * rank * width,
        PART,
        scratch=[pltpu.SemaphoreType.DMA((NZ,))],
    )(*panels)


def up_kernel(table, *refs):
    parts, panels, outs, low = refs[:NX], refs[NX], refs[NX + 1 : -1], refs[-1]
    for i in range(NZ):
        total = parts[0][i].astype(F32)
        for part in parts[1:]:
            total = total + part[i].astype(F32)
        low[i] = total.T
        picked = [
            low[i, pl.ds(pl.multiple_of(table[HOMES + r] * CAP, CAP), CAP), :]
            for r in range(COLUMNS)
        ]
        delta = jnp.dot(
            jnp.concatenate(picked, axis=0).astype(BF16), panels[i], preferred_element_type=F32
        ).astype(BF16)
        start = pl.multiple_of(table[ORDER + i] * CAP, CAP)
        for r in range(COLUMNS):
            outs[r][pl.ds(start, CAP), :] = delta[r * CAP : (r + 1) * CAP]


def up_step(table, parts, panels):
    _, rank, width = panels.shape
    lines = COLUMNS * CAP
    near = pl.BlockSpec(memory_space=pltpu.VMEM)
    return call(
        up_kernel,
        "up",
        [jax.ShapeDtypeStruct((NZ * CAP, width), BF16)] * COLUMNS,
        (1,),
        [near] * (NX + 1),
        [near] * COLUMNS,
        2 * NZ * lines * rank * width,
        2 * NZ * (lines + rank) * width,
        PART,
        prefetch=1,
        scratch=[pltpu.VMEM((NZ, lines, rank), F32)],
    )(table, *parts, panels)


def place_pieces(table, start, named, pieces):
    rows = pieces[0].shape[0]
    turn = lax.broadcasted_iota(jnp.int32, (named.shape[0], rows), 1)
    chosen = jnp.concatenate(
        [
            (turn + table[HANDLERS + start + r] * rows == named).astype(F32).astype(BF16)
            for r in range(len(pieces))
        ],
        axis=1,
    )
    delta = jnp.concatenate([piece[...] for piece in pieces], axis=0)
    return jnp.dot(chosen, delta, preferred_element_type=F32)


def early_kernel(start, table, place, base, *refs):
    pieces, out = refs[:-1], refs[-1]
    out[...] = base[...] + place_pieces(table, start, place[...], pieces)


def early_step(table, start, place, pieces, base):
    count = place.shape[0]
    rows, width = pieces[0].shape
    near = pl.BlockSpec(memory_space=pltpu.VMEM)
    return call(
        functools.partial(early_kernel, start),
        "early",
        jax.ShapeDtypeStruct((count, width), F32),
        (1,),
        [pl.BlockSpec((count, 1), lambda n, t: (0, 0))] + [near] * (1 + len(pieces)),
        near,
        2 * count * rows * len(pieces) * width,
        4 * count * width,
        PART,
        prefetch=1,
    )(table, place, base, *pieces)


def final_kernel(start, table, place, base, *refs):
    pieces, (out, made, sent) = refs[:-3], refs[-3:]
    count = made.shape[0]
    copies = []
    parts = sent.shape[0]
    tall = count // parts
    for part in range(parts):
        some = pl.ds(part * tall, tall)
        mine = place_pieces(table, start, place[some], pieces)
        made[some] = (base[some] + mine).astype(made.dtype)
        copy = pltpu.make_async_copy(made.at[some], out.at[some], sent.at[part])
        copy.start()
        copies.append(copy)
    for copy in copies:
        copy.wait()


def final_step(table, start, place, pieces, base):
    count = place.shape[0]
    rows, width = pieces[0].shape
    near = pl.BlockSpec(memory_space=pltpu.VMEM)
    return call(
        functools.partial(final_kernel, start),
        "final",
        jax.ShapeDtypeStruct((count, width), BF16),
        (1,),
        [near] * (2 + len(pieces)),
        pl.BlockSpec(memory_space=pltpu.HBM),
        2 * count * rows * len(pieces) * width,
        4 * count * width,
        PART,
        prefetch=1,
        scratch=[pltpu.VMEM((count, width), BF16), pltpu.SemaphoreType.DMA((2,))],
    )(table, place, base, *pieces)


def group_shift(dy, dc):
    return [
        (y * NC + core, (y + dy) % NY * NC + (core + dc) % NC)
        for y in range(NY)
        for core in range(NC)
    ]


def z_ring(chunk):
    fore = back = chunk
    found = [chunk]
    for step in range(1, 5):
        fore = lax.ppermute(fore, "z", ring(NZ, 1))
        found.append(fore)
        if step < 4:
            back = lax.ppermute(back, "z", ring(NZ, -1))
            found.append(back)
    return found


def on_device(tokens, owner, weight, down, up):
    z, y, core, x = (lax.axis_index(name) for name in ("z", "y", "core", "x"))
    count = tokens.shape[0]
    routes = ((0, 0),) + ROUTES
    table = jnp.stack(
        [(x + 2) % NX, (x + 1) % NX, (x + 3) % NX, x]
        + [(z + dz) % NZ for dz in RELATIVE_Z]
        + [(y + dy) % NY * NC + (core + dc) % NC for dy, dc in routes]
        + [(y - dy) % NY * NC + (core - dc) % NC for dy, dc in routes]
    )

    rows = lax.all_to_all(dispatch(tokens, owner), GROUP, 0, 0, tiled=True)
    panels = z_ring(jnp.concatenate([down[0], up[0]], axis=1))

    fore, back, ahead, sent = base_pair(tokens, weight, table, 0, (BF16, BF16, F32, BF16))
    tokens, fore, panels[1], panels[2] = lax.optimization_barrier(
        (tokens, fore, panels[1], panels[2])
    )
    given, behind, top, bottom = base_pair(tokens, weight, table, 2, (BF16, F32, F32, F32))
    fore = lax.ppermute(fore, "x", ring(NX, 1))
    back = lax.ppermute(back, "x", ring(NX, -1))
    fore_a = lax.ppermute(sent, "x", ring(NX, 1))
    back_a = lax.ppermute(given, "x", ring(NX, -1))
    fore_b = lax.ppermute((ahead + fore.astype(F32)).astype(BF16), "x", ring(NX, 1))
    back_b = lax.ppermute((behind + back.astype(F32)).astype(BF16), "x", ring(NX, -1))
    base = jnp.concatenate(
        [
            top + fore_b.astype(F32) + back_a.astype(F32),
            bottom + fore_a.astype(F32) + back_b.astype(F32),
        ],
        axis=0,
    )

    named = owner[:, 0]
    turn = jnp.arange(count, dtype=jnp.int32)
    earlier = (named[None, :] == named[:, None]) & (turn[None, :] < turn[:, None])
    position = jnp.sum(earlier.astype(jnp.int32), axis=1)
    place = (named % COLUMNS) * (NZ * CAP) + (named // COLUMNS) * CAP + position

    rows, base = lax.optimization_barrier((rows, base))
    part = down_step(table, rows, panels)
    parts = [part] + [lax.ppermute(part, "x", ring(NX, step)) for step in (2, 1, 3)]
    pieces = up_step(table, parts, collect(panels, up.shape[2]))
    pieces = [pieces[0]] + [
        lax.ppermute(piece, GROUP, group_shift(*route)) for piece, route in zip(pieces[1:], ROUTES)
    ]
    place = place[:, None]
    base = early_step(table, 0, place, pieces[:EARLY], base)
    return final_step(table, EARLY, place, pieces[EARLY:], base)


def solution(mesh):
    fine = Mesh(mesh.devices.reshape(NZ, NY, NC, NX), ("z", "y", "core", "x"))
    dp = ("z", "y", "core")
    placed = (P(dp, "x"), P(dp, None), P("x", None), P(dp, None, "x"), P(dp, None, "x"))
    return jax.shard_map(
        on_device, mesh=fine, in_specs=placed, out_specs=P(dp, "x"), check_vma=False
    )
```

```python
import functools

import jax
import jax.numpy as jnp
from jax import lax
from jax.experimental import pallas as pl
from jax.experimental.pallas import tpu as pltpu
from jax.sharding import Mesh, PartitionSpec as P

F32 = jnp.float32
BF16 = jnp.bfloat16
NZ, NY, NC, NX = 8, 4, 2, 4
COLUMNS = NY * NC
CAP = 16
EARLY = 7
GROUP = ("y", "core")
WHOLE, PART = 60, 16
ROUTES = ((2, 0), (2, 1), (1, 0), (3, 0), (0, 1), (1, 1), (3, 1))
RELATIVE_Z = (0, -1, 1, -2, 2, -3, 3, -4)
ORDER, HOMES, HANDLERS = 4, 12, 20


def ring(size, step):
    return [(place, (place + step) % size) for place in range(size)]


def call(kernel, name, out, grid, ins, outs, flops, moved, limit, prefetch=0, scratch=()):
    return pl.pallas_call(
        kernel,
        out_shape=out,
        grid_spec=pltpu.PrefetchScalarGridSpec(
            num_scalar_prefetch=prefetch,
            grid=grid,
            in_specs=ins,
            out_specs=outs,
            scratch_shapes=scratch,
        ),
        compiler_params=pltpu.CompilerParams(vmem_limit_bytes=limit * 1024 * 1024),
        cost_estimate=pl.CostEstimate(flops=flops, bytes_accessed=moved, transcendentals=0),
        name=name,
    )


def base_kernel(table, tokens, weight, *outs):
    product = jnp.dot(tokens[...], weight[...], preferred_element_type=F32)
    half = product.shape[0] // 2
    for j in range(2):

        @pl.when(pl.program_id(0) == j)
        def _():
            top, bottom = outs[2 * j : 2 * j + 2]
            top[...] = product[:half].astype(top.dtype)
            bottom[...] = product[half:].astype(bottom.dtype)


def base_pair(tokens, weight, table, start, types, tile=256):
    count, inner = tokens.shape
    width = weight.shape[1] // NX
    tiles = width // tile
    first = pl.BlockSpec((count // 2, tile), lambda j, n, w: (0, n + j * (tiles - 1 - n)))
    second = pl.BlockSpec((count // 2, tile), lambda j, n, w: (0, n * j))
    return call(
        base_kernel,
        "base",
        [jax.ShapeDtypeStruct((count // 2, width), kind) for kind in types],
        (2, tiles),
        [
            pl.BlockSpec((count, inner), lambda j, n, w: (0, 0)),
            pl.BlockSpec((inner, tile), lambda j, n, w: (0, w[start + j] * tiles + n)),
        ],
        [first, first, second, second],
        4 * count * inner * width,
        2 * (count + 2 * width) * inner,
        WHOLE,
        prefetch=1,
    )(table, tokens, weight)


def dispatch_kernel(owner, tokens, out, chosen, held, made, taken, given):
    count = held.shape[0]
    slots = chosen.shape[0]
    width = held.shape[1] // taken.shape[0]
    blocks = [pl.ds(part * width, width) for part in range(taken.shape[0])]
    fetches = [
        pltpu.make_async_copy(tokens.at[:, block], held.at[:, block], taken.at[part])
        for part, block in enumerate(blocks)
    ]
    for fetch in fetches:
        fetch.start()
    mine = owner[...]
    adapter = lax.broadcasted_iota(jnp.int32, (NZ * COLUMNS, count), 0)
    member = (adapter == mine).astype(F32)
    above = lax.broadcasted_iota(jnp.int32, (count, count), 0)
    below = lax.broadcasted_iota(jnp.int32, (count, count), 1)
    before = (above < below).astype(F32).astype(BF16)
    earlier = jnp.dot(member.astype(BF16), before, preferred_element_type=F32)
    position = jnp.sum(earlier * member, axis=0, keepdims=True).astype(jnp.int32)
    place = (mine % COLUMNS) * (NZ * CAP) + (mine // COLUMNS) * CAP + position
    slot = lax.broadcasted_iota(jnp.int32, (slots, count), 0)
    chosen[...] = (slot == place).astype(F32).astype(BF16)
    copies = []
    for part, block in enumerate(blocks):
        fetches[part].wait()
        product = jnp.dot(chosen[...], held[:, block], preferred_element_type=F32)
        made[:, :, block] = product.astype(BF16).reshape(made.shape[0], made.shape[1], width)
        copy = pltpu.make_async_copy(made.at[:, :, block], out.at[:, :, block], given.at[part])
        copy.start()
        copies.append(copy)
    for copy in copies:
        copy.wait()


def dispatch(tokens, owner):
    count, inner = tokens.shape
    rows = NZ * CAP
    whole = pl.BlockSpec(memory_space=pl.ANY)
    return call(
        dispatch_kernel,
        "dispatch",
        jax.ShapeDtypeStruct((COLUMNS, rows, inner), BF16),
        (1,),
        [pl.BlockSpec((1, count), lambda n: (0, 0)), whole],
        whole,
        2 * COLUMNS * rows * count * inner,
        2 * (count + COLUMNS * rows) * inner,
        WHOLE,
        scratch=[
            pltpu.VMEM((COLUMNS * rows, count), BF16),
            pltpu.VMEM((count, inner), BF16),
            pltpu.VMEM((COLUMNS, rows, inner), BF16),
            pltpu.SemaphoreType.DMA((4,)),
            pltpu.SemaphoreType.DMA((4,)),
        ],
    )(owner.reshape(1, count), tokens)


def down_kernel(table, rows, *refs):
    panels, (out, held, kept, first, second) = refs[:NZ], refs[NZ:]
    inner = rows.shape[2]
    copies = []
    for i in range(NZ):
        start = pl.multiple_of(table[ORDER + i] * CAP, CAP)
        pair = (
            pltpu.make_async_copy(rows.at[:, pl.ds(start, CAP), :], held.at[i], first.at[i]),
            pltpu.make_async_copy(panels[i].at[:, pl.ds(0, inner)], kept.at[i], second.at[i]),
        )
        for copy in pair:
            copy.start()
        copies.append(pair)
    many, rank = 4, kept.shape[1]
    lines = COLUMNS * CAP
    for start in range(0, NZ, many):
        for pair in copies[start : start + many]:
            for copy in pair:
                copy.wait()
        product = lax.dot_general(
            kept[start : start + many].reshape(many * rank, inner),
            held[start : start + many].reshape(many * lines, inner),
            (((1,), (1,)), ((), ())),
            preferred_element_type=F32,
        )
        for i in range(many):
            block = product[i * rank : (i + 1) * rank, i * lines : (i + 1) * lines]
            out[start + i] = block.astype(BF16)


def down_step(table, rows, panels):
    inner = rows.shape[2]
    rank = panels[0].shape[0]
    lines = COLUMNS * CAP
    whole = pl.BlockSpec(memory_space=pl.ANY)
    return call(
        down_kernel,
        "down",
        jax.ShapeDtypeStruct((NZ, rank, lines), BF16),
        (1,),
        [whole] * (1 + NZ),
        pl.BlockSpec(memory_space=pltpu.VMEM),
        2 * NZ * lines * inner * rank,
        2 * NZ * (lines + rank) * inner,
        PART,
        prefetch=1,
        scratch=[
            pltpu.VMEM((NZ, COLUMNS, CAP, inner), BF16),
            pltpu.VMEM((NZ, rank, inner), BF16),
            pltpu.SemaphoreType.DMA((NZ,)),
            pltpu.SemaphoreType.DMA((NZ,)),
        ],
    )(table, rows, *panels)


def collect_kernel(*refs):
    panels, (out, arrived) = refs[:NZ], refs[NZ:]
    width = out.shape[2]
    copies = [
        pltpu.make_async_copy(
            panels[i].at[:, pl.ds(panels[i].shape[1] - width, width)], out.at[i], arrived.at[i]
        )
        for i in range(NZ)
    ]
    for copy in copies:
        copy.start()
    for copy in copies:
        copy.wait()


def collect(panels, width):
    rank = panels[0].shape[0]
    return call(
        collect_kernel,
        "collect",
        jax.ShapeDtypeStruct((NZ, rank, width), BF16),
        (1,),
        [pl.BlockSpec(memory_space=pl.ANY)] * NZ,
        pl.BlockSpec(memory_space=pltpu.VMEM),
        0,
        4 * NZ * rank * width,
        PART,
        scratch=[pltpu.SemaphoreType.DMA((NZ,))],
    )(*panels)


def up_kernel(table, *refs):
    parts, panels, outs, low = refs[:NX], refs[NX], refs[NX + 1 : -1], refs[-1]
    for i in range(NZ):
        total = parts[0][i].astype(F32)
        for part in parts[1:]:
            total = total + part[i].astype(F32)
        low[i] = total.T
        picked = [
            low[i, pl.ds(pl.multiple_of(table[HOMES + r] * CAP, CAP), CAP), :]
            for r in range(COLUMNS)
        ]
        delta = jnp.dot(
            jnp.concatenate(picked, axis=0).astype(BF16), panels[i], preferred_element_type=F32
        ).astype(BF16)
        start = pl.multiple_of(table[ORDER + i] * CAP, CAP)
        for r in range(COLUMNS):
            outs[r][pl.ds(start, CAP), :] = delta[r * CAP : (r + 1) * CAP]


def up_step(table, parts, panels):
    _, rank, width = panels.shape
    lines = COLUMNS * CAP
    near = pl.BlockSpec(memory_space=pltpu.VMEM)
    return call(
        up_kernel,
        "up",
        [jax.ShapeDtypeStruct((NZ * CAP, width), BF16)] * COLUMNS,
        (1,),
        [near] * (NX + 1),
        [near] * COLUMNS,
        2 * NZ * lines * rank * width,
        2 * NZ * (lines + rank) * width,
        PART,
        prefetch=1,
        scratch=[pltpu.VMEM((NZ, lines, rank), F32)],
    )(table, *parts, panels)


def place_pieces(table, start, named, pieces):
    rows = pieces[0].shape[0]
    turn = lax.broadcasted_iota(jnp.int32, (named.shape[0], rows), 1)
    chosen = jnp.concatenate(
        [
            (turn + table[HANDLERS + start + r] * rows == named).astype(F32).astype(BF16)
            for r in range(len(pieces))
        ],
        axis=1,
    )
    delta = jnp.concatenate([piece[...] for piece in pieces], axis=0)
    return jnp.dot(chosen, delta, preferred_element_type=F32)


def early_kernel(start, table, place, base, *refs):
    pieces, out = refs[:-1], refs[-1]
    out[...] = base[...] + place_pieces(table, start, place[...], pieces)


def early_step(table, start, place, pieces, base):
    count = place.shape[0]
    rows, width = pieces[0].shape
    near = pl.BlockSpec(memory_space=pltpu.VMEM)
    return call(
        functools.partial(early_kernel, start),
        "early",
        jax.ShapeDtypeStruct((count, width), F32),
        (1,),
        [pl.BlockSpec((count, 1), lambda n, t: (0, 0))] + [near] * (1 + len(pieces)),
        near,
        2 * count * rows * len(pieces) * width,
        4 * count * width,
        PART,
        prefetch=1,
    )(table, place, base, *pieces)


def final_kernel(start, table, place, base, *refs):
    pieces, (out, made, sent) = refs[:-3], refs[-3:]
    count = made.shape[0]
    copies = []
    parts = sent.shape[0]
    tall = count // parts
    for part in range(parts):
        some = pl.ds(part * tall, tall)
        mine = place_pieces(table, start, place[some], pieces)
        made[some] = (base[some] + mine).astype(made.dtype)
        copy = pltpu.make_async_copy(made.at[some], out.at[some], sent.at[part])
        copy.start()
        copies.append(copy)
    for copy in copies:
        copy.wait()


def final_step(table, start, place, pieces, base):
    count = place.shape[0]
    rows, width = pieces[0].shape
    near = pl.BlockSpec(memory_space=pltpu.VMEM)
    return call(
        functools.partial(final_kernel, start),
        "final",
        jax.ShapeDtypeStruct((count, width), BF16),
        (1,),
        [near] * (2 + len(pieces)),
        pl.BlockSpec(memory_space=pltpu.HBM),
        2 * count * rows * len(pieces) * width,
        4 * count * width,
        PART,
        prefetch=1,
        scratch=[pltpu.VMEM((count, width), BF16), pltpu.SemaphoreType.DMA((2,))],
    )(table, place, base, *pieces)


def group_shift(dy, dc):
    return [
        (y * NC + core, (y + dy) % NY * NC + (core + dc) % NC)
        for y in range(NY)
        for core in range(NC)
    ]


def z_ring(chunk):
    fore = back = chunk
    found = [chunk]
    for step in range(1, 5):
        fore = lax.ppermute(fore, "z", ring(NZ, 1))
        found.append(fore)
        if step < 4:
            back = lax.ppermute(back, "z", ring(NZ, -1))
            found.append(back)
    return found


def on_device(tokens, owner, weight, down, up):
    z, y, core, x = (lax.axis_index(name) for name in ("z", "y", "core", "x"))
    count = tokens.shape[0]
    routes = ((0, 0),) + ROUTES
    table = jnp.stack(
        [(x + 2) % NX, (x + 1) % NX, (x + 3) % NX, x]
        + [(z + dz) % NZ for dz in RELATIVE_Z]
        + [(y + dy) % NY * NC + (core + dc) % NC for dy, dc in routes]
        + [(y - dy) % NY * NC + (core - dc) % NC for dy, dc in routes]
    )

    rows = lax.all_to_all(dispatch(tokens, owner), GROUP, 0, 0, tiled=True)
    panels = z_ring(jnp.concatenate([down[0], up[0]], axis=1))

    fore, back, ahead, sent = base_pair(tokens, weight, table, 0, (BF16, BF16, F32, BF16))
    tokens, fore, panels[1], panels[2] = lax.optimization_barrier(
        (tokens, fore, panels[1], panels[2])
    )
    given, behind, top, bottom = base_pair(tokens, weight, table, 2, (BF16, F32, F32, F32))
    fore = lax.ppermute(fore, "x", ring(NX, 1))
    back = lax.ppermute(back, "x", ring(NX, -1))
    fore_a = lax.ppermute(sent, "x", ring(NX, 1))
    back_a = lax.ppermute(given, "x", ring(NX, -1))
    fore_b = lax.ppermute((ahead + fore.astype(F32)).astype(BF16), "x", ring(NX, 1))
    back_b = lax.ppermute((behind + back.astype(F32)).astype(BF16), "x", ring(NX, -1))
    base = jnp.concatenate(
        [
            top + fore_b.astype(F32) + back_a.astype(F32),
            bottom + fore_a.astype(F32) + back_b.astype(F32),
        ],
        axis=0,
    )

    named = owner[:, 0]
    turn = jnp.arange(count, dtype=jnp.int32)
    earlier = (named[None, :] == named[:, None]) & (turn[None, :] < turn[:, None])
    position = jnp.sum(earlier.astype(jnp.int32), axis=1)
    place = (named % COLUMNS) * (NZ * CAP) + (named // COLUMNS) * CAP + position

    rows, base = lax.optimization_barrier((rows, base))
    part = down_step(table, rows, panels)
    parts = [part] + [lax.ppermute(part, "x", ring(NX, step)) for step in (2, 1, 3)]
    pieces = up_step(table, parts, collect(panels, up.shape[2]))
    pieces = [pieces[0]] + [
        lax.ppermute(piece, GROUP, group_shift(*route)) for piece, route in zip(pieces[1:], ROUTES)
    ]
    place = place[:, None]
    base = early_step(table, 0, place, pieces[:EARLY], base)
    return final_step(table, EARLY, place, pieces[EARLY:], base)


def solution(mesh):
    fine = Mesh(mesh.devices.reshape(NZ, NY, NC, NX), ("z", "y", "core", "x"))
    dp = ("z", "y", "core")
    placed = (P(dp, "x"), P(dp, None), P("x", None), P(dp, None, "x"), P(dp, None, "x"))
    return jax.shard_map(
        on_device, mesh=fine, in_specs=placed, out_specs=P(dp, "x"), check_vma=False
    )
```
